32 devices in a mesh: pre: 2 (over y), dec: 4 (over x, core), rep: 4 (over z).
Axes of the slice: x: 2, y: 2, z: 4, core: 2. Of those that a mesh axis runs over, the one named last changes fastest.
Arguments:
- layer_queries: bfloat16 [2048, 8192], P(('pre', 'rep'), 'dec'), may hold values from -16 to 16
- layer_keys: bfloat16 [2048, 1024], P(('pre', 'rep')), may hold values from -16 to 16
- layer_values: bfloat16 [2048, 1024], P(('pre', 'rep')), may hold values from -6 to 6
- query_bias: float32 [8192], P('dec'), may hold values from -3 to 3
- key_bias: float32 [1024], replicated, may hold values from -3 to 3
- value_bias: float32 [1024], replicated, may hold values from -3 to 3
- positions: int32 [2048], replicated, may hold values from 0 to 2047, each once
- lengths: int32 [32], replicated, may hold values from 1 to 1024, as said below
- replica_of: int32 [32], replicated, may hold values from 0 to 3, as said below
- page_table: int32 [4, 16], replicated, may hold values from 0 to 3, as said below
- prefill_cache: bfloat16 [4, 16, 16, 4, 64, 128], P('rep', 'pre', 'dec'), may hold values from -6 to 6
Outputs:
- context: bfloat16 [2048, 8192], P(('pre', 'rep'), 'dec')
- decode_cache: bfloat16 [4, 4, 8, 16, 4, 64, 128], P('rep', 'dec', None, 'pre')
The draws below stay inside these ranges and needn't reach their ends.
Inputs may be any that keep to these rules, and one draw needn't show every extreme that they name: `replica_of`: each replica receives exactly 8 requests. `lengths`: the requests of each replica fill exactly 16 blocks of 128 tokens, each request starting a new block; in each replica one request spans exactly 8 full blocks. `page_table`: in each aligned run of 8 blocks of a replica, exactly half of the 4 decode devices appear, each exactly 4 times.
All inputs are finite; a program needn't handle non-finite values.
Results may differ from the reference program's by a relative error of at most 0.0094.
Values may be sent and summed in bfloat16 or wider, within the bound.
No kernel may reach another device: no remote copies, remote signals or barrier semaphores. Data moves between devices by JAX's collectives and lax.ppermute only.
A program may use at most 128 MiB of HBM per device.

```python
import jax
import jax.numpy as jnp
from jax import lax

HEADS = 64
KVH = 8
HD = 128
BLOCK = 128
LKV = 4
REQ_REP = 8
BLK_SRC = 8
TOKENS = 2048
REPLICAS = 4
DECODERS = 4
RUNS = 2
HALF = 64
HALVES = 16
CAP = 4
SLOTS = 8
BLK_REP = 16
MOST_BLK = 8
REQS = 32


def handover_plan(key):
    order = jax.random.permutation(jax.random.fold_in(key, 1), REQS)
    replica_of = (order % REPLICAS).astype(jnp.int32)
    request_ids = jnp.arange(REQS, dtype=jnp.int32)
    same = replica_of[None, :] == replica_of[:, None]
    ranks = jnp.sum(same & (request_ids[None, :] < request_ids[:, None]), axis=1).astype(jnp.int32)
    remain = BLK_REP - MOST_BLK

    def replica_counts(sub):
        cuts = jnp.sort(jax.random.permutation(jax.random.fold_in(sub, 1), remain - 1)[:REQ_REP - 2] + 1)
        edges = jnp.concatenate([jnp.zeros((1,), jnp.int32), cuts.astype(jnp.int32), jnp.full((1,), remain, jnp.int32)])
        pieces = edges[1:] - edges[:-1]
        longest = jax.random.randint(jax.random.fold_in(sub, 2), (), 0, REQ_REP)
        places = jnp.arange(REQ_REP, dtype=jnp.int32)
        moved = jnp.clip(places - (places > longest).astype(jnp.int32), 0, REQ_REP - 2)
        return (jnp.where(places == longest, MOST_BLK, pieces[moved]).astype(jnp.int32), longest)
    subkeys = jax.random.split(jax.random.fold_in(key, 2), REPLICAS)
    counts, longest = jax.vmap(replica_counts)(subkeys)
    request_blocks = counts[replica_of, ranks]
    tails = jax.random.randint(jax.random.fold_in(key, 3), (REQS,), 1, BLOCK + 1)
    tails = jnp.where(ranks == longest[replica_of], BLOCK, tails)
    lengths = (BLOCK * (request_blocks - 1) + tails).astype(jnp.int32)

    def hot_order(sub):
        return jax.random.permutation(sub, DECODERS)
    hot_rank = jax.vmap(hot_order)(jax.random.split(jax.random.fold_in(key, 4), REPLICAS))
    hotter = (hot_rank < DECODERS // 4).astype(jnp.int32)
    noise = jax.random.randint(jax.random.fold_in(key, 5), (REPLICAS, RUNS, DECODERS), 0, 1000)
    ranking = (noise + 700 * hotter[:, None, :]) * DECODERS + jnp.arange(DECODERS, dtype=jnp.int32)
    chosen = lax.top_k(ranking, DECODERS // 2)[1].astype(jnp.int32)
    listed = jnp.repeat(chosen, CAP, axis=2)
    shuffle = jax.random.randint(jax.random.fold_in(key, 6), (REPLICAS, RUNS, BLK_SRC), 0, 1 << 20) * BLK_SRC + jnp.arange(BLK_SRC, dtype=jnp.int32)
    reorder = jnp.argsort(shuffle, axis=2, stable=True)
    page_table = jnp.take_along_axis(listed, reorder, axis=2).reshape(REPLICAS, BLK_REP).astype(jnp.int32)
    return (lengths, replica_of, page_table)


def draw_lengths(key, part):
    return handover_plan(jax.random.fold_in(key, 11))[0]


def draw_replica_of(key, part):
    return handover_plan(jax.random.fold_in(key, 11))[1]


def draw_page_table(key, part):
    return handover_plan(jax.random.fold_in(key, 11))[2]


def draw_layer_queries(key, part):
    base = jnp.clip(jax.random.normal(jax.random.fold_in(key, 2), (TOKENS, HEADS, HD)) * 2.5, -10.0, 10.0)
    return base.reshape(TOKENS, HEADS * HD).astype(jnp.bfloat16)


def draw_layer_keys(key, part):
    base = jnp.clip(jax.random.normal(jax.random.fold_in(key, 4), (TOKENS, KVH, HD)), -4.0, 4.0)
    return base.reshape(TOKENS, KVH * HD).astype(jnp.bfloat16)


def shard_levels(own_key, shape, cuts, smallest, top_value):
    factor_of = 1.0
    for dim, shards_of in cuts:
        steps = jax.random.uniform(jax.random.fold_in(jax.random.fold_in(own_key, 6), dim), (shards_of,), jnp.float32, smallest / len(cuts), top_value / len(cuts))
        factor_of = factor_of * jnp.repeat(jnp.exp(steps), shape[dim] // shards_of).reshape((-1,) + (1,) * (len(shape) - 1 - dim))
    return factor_of


def scatter_about(key, extent, scale, limit, cuts=(), kind=jnp.bfloat16):
    loudness = shard_levels(key, extent, cuts, -0.22, 0.18) if cuts else 1.0
    drawn = jax.random.normal(key, extent, jnp.float32) * scale * loudness
    return jnp.minimum(jnp.maximum(drawn, -limit), limit).astype(kind)


def setup_inputs(seed: int = 0) -> dict:
    arg_keys = jax.random.split(jax.random.key(seed), 12)
    return {
        "layer_queries": draw_layer_queries(jax.random.fold_in(arg_keys[11], 71), 0),
        "layer_keys": draw_layer_keys(jax.random.fold_in(arg_keys[11], 71), 0),
        "layer_values": scatter_about(arg_keys[2], (TOKENS, KVH * HD), 1.0, 6.0, ((0, 8),)),
        "query_bias": scatter_about(arg_keys[3], (HEADS * HD,), 0.5, 3.0, ((0, 4),), jnp.float32),
        "key_bias": scatter_about(arg_keys[4], (KVH * HD,), 0.5, 3.0, (), jnp.float32),
        "value_bias": scatter_about(arg_keys[5], (KVH * HD,), 0.5, 3.0, (), jnp.float32),
        "positions": jax.random.permutation(arg_keys[6], TOKENS).astype(jnp.int32),
        "lengths": draw_lengths(jax.random.fold_in(arg_keys[11], 71), 0),
        "replica_of": draw_replica_of(jax.random.fold_in(arg_keys[11], 71), 0),
        "page_table": draw_page_table(jax.random.fold_in(arg_keys[11], 71), 0),
        "prefill_cache": scatter_about(arg_keys[10], (REPLICAS, BLK_REP, HALVES, LKV, HALF, BLOCK), 1.0, 6.0, ((0, 4), (1, 2), (2, 4))),
    }


rope_base = 1000000.0


def rotate(values, where_at):
    width = values.shape[-1]
    half_width = width // 2
    freqs = 1.0 / (rope_base ** (jnp.arange(half_width, dtype=jnp.float32) * (2.0 / width)))
    angles = where_at.astype(jnp.float32)[:, None] * freqs[None, :]
    cosine = jnp.cos(angles)[:, None, :]
    sine = jnp.sin(angles)[:, None, :]
    first = values[..., :half_width]
    second = values[..., half_width:]
    return jnp.concatenate([first * cosine - second * sine, second * cosine + first * sine], axis=-1)


def valid_tokens(lengths, replica_of, replica, block_ids):
    member = replica_of == replica
    counts = jnp.where(member, (lengths + (BLOCK - 1)) // BLOCK, 0).astype(jnp.int32)
    starts = (jnp.cumsum(counts) - counts).astype(jnp.int32)
    inside = (block_ids[:, None] >= starts[None, :]) & (block_ids[:, None] < (starts + counts)[None, :])
    remain = lengths[None, :] - BLOCK * (block_ids[:, None] - starts[None, :])
    return jnp.sum(jnp.where(inside, jnp.clip(remain, 0, BLOCK), 0), axis=1).astype(jnp.int32)


def reference(layer_queries, layer_keys, layer_values, query_bias, key_bias, value_bias, positions, lengths, replica_of, page_table, prefill_cache):
    token_count = layer_queries.shape[0]
    scale = HD ** -0.5
    group_size = HEADS // KVH
    shifted = layer_queries.astype(jnp.float32).reshape(token_count, HEADS, HD) + query_bias.reshape(HEADS, HD)
    query_rot = rotate(shifted, positions).astype(jnp.bfloat16)
    shifted_keys = layer_keys.astype(jnp.float32).reshape(token_count, KVH, HD) + key_bias.reshape(KVH, HD)
    key_rot = rotate(shifted_keys, positions).astype(jnp.bfloat16)
    value_all = (layer_values.astype(jnp.float32).reshape(token_count, KVH, HD) + value_bias.reshape(KVH, HD)).astype(jnp.bfloat16)
    allowed = positions[None, :] <= positions[:, None]

    def one_head(head):
        shared = (head // group_size).astype(jnp.int32)
        head_queries = lax.dynamic_index_in_dim(query_rot, head, 1, keepdims=False)
        head_keys = lax.dynamic_index_in_dim(key_rot, shared, 1, keepdims=False)
        head_values = lax.dynamic_index_in_dim(value_all, shared, 1, keepdims=False)
        scores = jnp.dot(head_queries, head_keys.T, preferred_element_type=jnp.float32) * scale
        scores = jnp.where(allowed, scores, -jnp.inf)
        highest = jnp.max(scores, axis=1, keepdims=True)
        weights = jnp.exp(scores - highest)
        total = jnp.sum(weights, axis=1, keepdims=True)
        summed = jnp.dot(weights.astype(jnp.bfloat16), head_values, preferred_element_type=jnp.float32)
        return (summed / total).astype(jnp.bfloat16)

    per_head = lax.map(one_head, jnp.arange(HEADS, dtype=jnp.int32))
    context = jnp.transpose(per_head, (1, 0, 2)).reshape(token_count, HEADS * HD)

    block_ids = jnp.arange(BLK_REP, dtype=jnp.int32)
    run_of = block_ids // BLK_SRC
    earlier = block_ids[None, :] < block_ids[:, None]
    pools = []
    for replica in range(REPLICAS):
        valid = valid_tokens(lengths, replica_of, replica, block_ids)
        keep = (jnp.arange(BLOCK, dtype=jnp.int32)[None, :] < valid[:, None]).astype(jnp.bfloat16)
        masked = prefill_cache[replica] * keep[:, None, None, None, :]
        target = page_table[replica].astype(jnp.int32)
        same = (target[None, :] == target[:, None]) & (run_of[None, :] == run_of[:, None]) & earlier
        slot = (run_of * CAP + jnp.sum(same, axis=1)).astype(jnp.int32)
        pool = jnp.zeros((DECODERS, SLOTS) + masked.shape[1:], jnp.bfloat16).at[target, slot].set(masked)
        pools.append(pool)
    decode_cache = jnp.stack(pools)
    return context, decode_cache
```

```python
import functools

import jax
import jax.numpy as jnp
import numpy as np
from jax import lax
from jax.experimental import pallas as pl
from jax.experimental.pallas import tpu as pltpu
from jax.sharding import PartitionSpec as P

HEADS = 64
KVH = 8
HD = 128
BLOCK = 128

rope_base = 1000000.0
masked_score = -1e30
log2_e = 1.4426950408889634

ANY = pl.BlockSpec(memory_space=pl.ANY)
SMEM = pl.BlockSpec(memory_space=pltpu.SMEM)
VMEM = pl.BlockSpec(memory_space=pltpu.VMEM)
SMALL = pl.CostEstimate(flops=1, bytes_accessed=1, transcendentals=0)


def row_freqs():
    lane = np.arange(HD) % (HD // 2)
    freqs = 1.0 / rope_base ** (lane * (2.0 / HD))
    return jnp.asarray(freqs.astype(np.float32).reshape(1, HD))


def rotate(values, cosine, sine):
    return values * cosine + pltpu.roll(values, HD // 2, 1) * sine


def turn_kernel(
    dims,
    pos_ref,
    freq_ref,
    key_bias_ref,
    value_bias_ref,
    keys_hbm,
    values_hbm,
    kv_ref,
    cos_ref,
    sin_ref,
    qpos_ref,
    keys_buf,
    values_buf,
    sems,
):
    kv_local, head_count, rows, rep_size = dims
    pre, dec, rep = lax.axis_index("pre"), lax.axis_index("dec"), lax.axis_index("rep")
    kv_first = dec * head_count // (HEADS // KVH)
    columns = pl.ds(pl.multiple_of(kv_first * HD, HD), kv_local * HD)
    keys_in = pltpu.make_async_copy(keys_hbm.at[:, columns], keys_buf, sems.at[0])
    values_in = pltpu.make_async_copy(values_hbm.at[:, columns], values_buf, sems.at[1])
    keys_in.start()
    values_in.start()
    first = (pre * rep_size + rep) * (rows // HD)
    lanes = lax.broadcasted_iota(jnp.int32, (HD, HD), 1)
    for r in range(rows // HD):
        part = slice(r * HD, (r + 1) * HD)
        row = pos_ref[pl.ds(first + r, 1), :]
        column = jnp.broadcast_to(row, (HD, HD)).astype(jnp.float32).T
        qpos_ref[part, :] = column.astype(jnp.int32)
        angle = column * freq_ref[...]
        sine = jnp.sin(angle)
        cos_ref[part, :] = jnp.cos(angle)
        sin_ref[part, :] = jnp.where(lanes < HD // 2, -sine, sine)
    keys_in.wait()
    values_in.wait()
    for g in range(kv_local):
        where = pl.ds(pl.multiple_of((kv_first + g) * HD, HD), HD)
        part = slice(g * HD, (g + 1) * HD)
        shifted = keys_buf[:, part].astype(jnp.float32) + key_bias_ref[:, where]
        turned = rotate(shifted, cos_ref[...], sin_ref[...]).astype(jnp.bfloat16)
        biased = values_buf[:, part].astype(jnp.float32) + value_bias_ref[:, where]
        biased = biased.astype(jnp.bfloat16)
        kv_ref[0, g] = turned
        kv_ref[1, g] = biased


def turn(dims, positions, key_bias, value_bias, keys, values):
    kv_local, head_count, rows, rep_size = dims
    return pl.pallas_call(
        functools.partial(turn_kernel, dims),
        out_shape=[
            jax.ShapeDtypeStruct((2, kv_local, rows, HD), jnp.bfloat16),
            jax.ShapeDtypeStruct((rows, HD), jnp.float32),
            jax.ShapeDtypeStruct((rows, HD), jnp.float32),
            jax.ShapeDtypeStruct((rows, HD), jnp.int32),
        ],
        in_specs=[VMEM] * 4 + [ANY] * 2,
        out_specs=[VMEM] * 4,
        scratch_shapes=[
            pltpu.VMEM((rows, kv_local * HD), jnp.bfloat16),
            pltpu.VMEM((rows, kv_local * HD), jnp.bfloat16),
            pltpu.SemaphoreType.DMA((2,)),
        ],
        cost_estimate=SMALL,
        name="turn",
    )(
        positions.reshape(-1, HD),
        row_freqs(),
        key_bias.reshape(1, -1),
        value_bias.reshape(1, -1),
        keys,
        values,
    )


def pack_kernel(dims, page_ref, lengths_ref, replica_ref, kv_hbm, cache_hbm, *rest):
    blk_count, group, dec_size = dims
    sends = rest[:dec_size]
    held, valid, counts, in_sems, out_sems = rest[dec_size:]
    pre, dec, rep = lax.axis_index("pre"), lax.axis_index("dec"), lax.axis_index("rep")
    blocks_in = [
        pltpu.make_async_copy(cache_hbm.at[0, b], held.at[b], in_sems.at[b])
        for b in range(blk_count)
    ]
    for copy in blocks_in:
        copy.start()
    blocks_all = valid.shape[0]
    for k in range(blocks_all):
        valid[k] = 0
    for d in range(dec_size):
        counts[d] = 0

    def request(i, start):
        mine = replica_ref[i] == rep
        length = lengths_ref[i]
        number = jnp.where(mine, (length + (BLOCK - 1)) // BLOCK, 0)

        def block(k, carry):
            valid[start + k] = jnp.minimum(BLOCK, length - BLOCK * k)
            return carry

        lax.fori_loop(0, jnp.minimum(number, blocks_all - start), block, 0)
        return start + number

    lax.fori_loop(0, lengths_ref.shape[0], request, 0)
    place = pre * group + dec % group
    lane = lax.broadcasted_iota(jnp.int32, held.shape[1:], len(held.shape) - 2)
    for b in range(blk_count):
        k = pre * blk_count + b
        blocks_in[b].wait()
        limit = valid[k]

        @pl.when(limit < BLOCK)
        def _(b=b, limit=limit):
            held[b] = jnp.where(lane < limit, held[b], jnp.zeros_like(held[b]))

        target = page_ref[rep, k]
        rank = counts[target]
        counts[target] = rank + 1
        for j in range(dec_size):

            @pl.when(target == (place ^ j))
            def _(b=b, j=j, rank=rank):
                pltpu.make_async_copy(held.at[b], sends[j].at[rank], out_sems.at[b]).start()

    for b in range(blk_count):
        pltpu.make_async_copy(held.at[b], sends[0].at[0], out_sems.at[b]).wait()


def pack(dims, capacity, page_table, lengths, replica_of, kv, cache):
    blk_count, group, dec_size = dims
    block = cache.shape[2:]
    return pl.pallas_call(
        functools.partial(pack_kernel, dims),
        out_shape=[jax.ShapeDtypeStruct((capacity,) + block, jnp.bfloat16)] * dec_size,
        in_specs=[SMEM] * 3 + [ANY] * 2,
        out_specs=[ANY] * dec_size,
        scratch_shapes=[
            pltpu.VMEM((blk_count,) + block, jnp.bfloat16),
            pltpu.SMEM((page_table.shape[1],), jnp.int32),
            pltpu.SMEM((dec_size,), jnp.int32),
            pltpu.SemaphoreType.DMA((blk_count,)),
            pltpu.SemaphoreType.DMA((blk_count,)),
        ],
        cost_estimate=SMALL,
        name="pack",
    )(page_table, lengths, replica_of, kv, cache)


def after(value, *before):
    return lax.optimization_barrier((value,) + before)[0] if before else value


def query_kernel(query_ref, bias_ref, cos_ref, sin_ref, out_ref):
    for h in range(out_ref.shape[0]):
        columns = slice(h * HD, (h + 1) * HD)
        shifted = query_ref[:, columns].astype(jnp.float32) + bias_ref[:, columns]
        out_ref[h] = rotate(shifted, cos_ref[...], sin_ref[...]).astype(jnp.bfloat16)


def rotate_queries(queries, bias, cosine, sine):
    rows, columns = queries.shape
    return pl.pallas_call(
        query_kernel,
        out_shape=jax.ShapeDtypeStruct((columns // HD, rows, HD), jnp.bfloat16),
        in_specs=[VMEM] * 4,
        out_specs=VMEM,
        cost_estimate=SMALL,
        name="rotate_queries",
    )(queries, bias.reshape(1, -1), cosine, sine)


def attend_kernel(moves, rep_size, first, last, query_ref, qpos_ref, pos_ref, *rest):
    chunks, rest = rest[: len(moves)], rest[len(moves) :]
    if not first:
        stat_in, sum_in, rest = rest[0], rest[1], rest[2:]
    outs = rest
    step_heads, rows, _ = query_ref.shape
    half = HD // 2
    pre, rep = lax.axis_index("pre"), lax.axis_index("rep")
    scale = HD ** (-0.5) * log2_e
    qpos = qpos_ref[:, :1]
    lanes = lax.broadcasted_iota(jnp.int32, (rows, HD), 1)
    bias, keys, values = [], [], []
    for (move_pre, move_rep), chunk in zip(moves, chunks):
        block = (pre ^ move_pre) * rep_size + (rep ^ move_rep)
        parts = [pos_ref[pl.ds(block * (rows // HD) + r, 1), :] for r in range(rows // HD)]
        bias.append(jnp.concatenate(parts, axis=1) <= qpos)
        keys.append(chunk[0, 0])
        values.append(jnp.concatenate([chunk[1, 0], jnp.ones((rows, HD), jnp.bfloat16)], axis=1))
    stat = jnp.zeros((rows, HD), jnp.float32)
    for h in range(step_heads):
        query = query_ref[h]
        scores = []
        for allowed, key in zip(bias, keys):
            product = lax.dot_general(
                query, key, (((1,), (1,)), ((), ())), preferred_element_type=jnp.float32
            )
            scores.append(jnp.where(allowed, product, masked_score))
        newest = jnp.max(functools.reduce(jnp.maximum, scores), axis=1, keepdims=True)
        if not first:
            best = stat_in[0, :, h : h + 1]
            newest = jnp.maximum(newest, best)
            decay = jnp.exp2((best - newest) * scale)
        both = 0.0
        for score, value in zip(scores, values):
            weights = jnp.exp2((score - newest) * scale)
            both = both + jnp.dot(
                weights.astype(jnp.bfloat16), value, preferred_element_type=jnp.float32
            )
        added, total = both[:, :HD], both[:, HD:]
        if not first:
            total = total + stat_in[0, :, half + h : half + h + 1] * decay
            added = added + sum_in[h] * decay
        if last:
            outs[0][:, h * HD : (h + 1) * HD] = (added / total).astype(jnp.bfloat16)
        else:
            stat = jnp.where(lanes == h, newest, jnp.where(lanes == half + h, total, stat))
            outs[1][h] = added
    if not last:
        outs[0][0] = stat


def attend(pairs, rep_size, per_group, queries, qpos, positions, state, last):
    heads, rows, _ = queries.shape
    step_heads = per_group
    first = state is None
    moves, chunks = zip(*pairs)
    whole = lambda i: (0, 0)
    by_head = pl.BlockSpec((step_heads, rows, HD), lambda i: (i, 0, 0))
    by_step = pl.BlockSpec((1, rows, HD), lambda i: (i, 0, 0))
    chunk_spec = pl.BlockSpec((2, 1, rows, HD), lambda i: (0, i, 0, 0))
    pos2 = positions.reshape(-1, HD)
    in_specs = (
        [by_head, pl.BlockSpec((rows, HD), whole), pl.BlockSpec(pos2.shape, whole)]
        + [chunk_spec] * len(chunks)
        + ([] if first else [by_step, by_head])
    )
    if last:
        out_shape = jax.ShapeDtypeStruct((rows, heads * HD), jnp.bfloat16)
        out_specs = pl.BlockSpec((rows, step_heads * HD), lambda i: (0, i))
    else:
        out_shape = [
            jax.ShapeDtypeStruct((heads // step_heads, rows, HD), jnp.float32),
            jax.ShapeDtypeStruct((heads, rows, HD), jnp.float32),
        ]
        out_specs = [by_step, by_head]
    return pl.pallas_call(
        functools.partial(attend_kernel, moves, rep_size, first, last),
        grid=(heads // step_heads,),
        out_shape=out_shape,
        in_specs=in_specs,
        out_specs=out_specs,
        compiler_params=pltpu.CompilerParams(vmem_limit_bytes=40 << 20),
        cost_estimate=SMALL,
        name="attend",
    )(queries, qpos, pos2, *chunks, *(() if first else state))


def place_kernel(dims, here, rest_j, page_ref, own_hbm, *rest):
    blk_count, capacity, hl, group = dims
    arrived, rest = rest[: len(here)], rest[len(here) :]
    out_hbm, held, zeros, in_sems, out_sems = rest[-5:]
    pre, dec, rep = lax.axis_index("pre"), lax.axis_index("dec"), lax.axis_index("rep")

    def goal(j):
        source = dec ^ j
        run, part = source // group, source % group
        used = functools.reduce(
            jnp.logical_or,
            [page_ref[rep, run * blk_count + b] == dec for b in range(blk_count)],
        )
        return used, lambda c: out_hbm.at[0, 0, run * capacity + c, pl.ds(part * hl, hl)]

    moves = []
    for n, j in enumerate(here):
        used, to = goal(j)
        for c in range(capacity):
            inward = pltpu.make_async_copy(arrived[n].at[c], held.at[n, c], in_sems.at[n, c])
            outward = pltpu.make_async_copy(held.at[n, c], to(c), out_sems.at[n, c])
            moves.append((used, inward, outward))
            local = used & (dec // group == pre) if j == 0 else None
            if j == 0:
                kept = pltpu.make_async_copy(own_hbm.at[c], held.at[n, c], in_sems.at[n, c])

                @pl.when(local)
                def _(kept=kept):
                    kept.start()

            @pl.when(used if local is None else used & jnp.logical_not(local))
            def _(inward=inward):
                inward.start()

    fills = []
    if rest_j:
        zeros[...] = jnp.zeros_like(zeros)
        for n, j in enumerate(rest_j):
            used, to = goal(j)
            for c in range(capacity):
                fill = pltpu.make_async_copy(zeros, to(c), out_sems.at[len(here) + n, c])
                fills.append((used, fill))

                @pl.when(jnp.logical_not(used))
                def _(fill=fill):
                    fill.start()

    for used, inward, outward in moves:

        @pl.when(used)
        def _(inward=inward, outward=outward):
            inward.wait()
            outward.start()

    for used, inward, outward in moves:

        @pl.when(used)
        def _(outward=outward):
            outward.wait()

    for used, fill in fills:

        @pl.when(jnp.logical_not(used))
        def _(fill=fill):
            fill.wait()


def place(dims, pre_size, here, rest_j, page_table, own, arrived, buffer):
    blk_count, capacity, hl, group = dims
    block = arrived[0].shape[2:]
    count = len(here)
    kept = [] if buffer is None else [buffer]
    return pl.pallas_call(
        functools.partial(place_kernel, dims, here, rest_j),
        out_shape=jax.ShapeDtypeStruct((1, 1, pre_size * capacity, group * hl) + block, jnp.bfloat16),
        in_specs=[SMEM] + [ANY] * (1 + count + len(kept)),
        out_specs=ANY,
        scratch_shapes=[
            pltpu.VMEM((count, capacity, hl) + block, jnp.bfloat16),
            pltpu.VMEM((hl,) + block, jnp.bfloat16),
            pltpu.SemaphoreType.DMA((count, capacity)),
            pltpu.SemaphoreType.DMA((count + len(rest_j), capacity)),
        ],
        input_output_aliases={2 + count: 0} if kept else {},
        cost_estimate=SMALL,
        name="place",
    )(page_table, own, *arrived, *kept)


def shards(
    layer_queries,
    layer_keys,
    layer_values,
    query_bias,
    key_bias,
    value_bias,
    positions,
    lengths,
    replica_of,
    page_table,
    prefill_cache,
):
    pre_size, dec_size, rep_size = (lax.axis_size(a) for a in ("pre", "dec", "rep"))
    rows = layer_queries.shape[0]
    head_count = layer_queries.shape[1] // HD
    group_size = HEADS // KVH
    kv_local = max(1, head_count // group_size)
    per_group = head_count // kv_local
    blk_count, hl = prefill_cache.shape[1], prefill_cache.shape[2]
    capacity = 2 * blk_count // dec_size
    group = dec_size // pre_size
    kv, cosine, sine, qpos = turn(
        (kv_local, head_count, rows, rep_size), positions, key_bias, value_bias,
        layer_keys, layer_values,
    )
    sends = pack((blk_count, group, dec_size), capacity, page_table, lengths, replica_of, kv, prefill_cache)
    swap = lambda value, axis, size, hop: lax.ppermute(
        value, axis, [(i, i ^ hop) for i in range(size)]
    )
    near = [kv] + [swap(kv, "pre", pre_size, s) for s in range(1, pre_size)]
    arrived = {}

    def hand_over(j, *before):
        route = []
        for p in range(pre_size):
            for d in range(dec_size):
                goal = (p * group + d % group) ^ j
                pair = (p * dec_size + d, (d // group) * dec_size + goal)
                if pair[0] != pair[1]:
                    route.append(pair)
        arrived[j] = lax.ppermute(after(sends[j], *before), ("pre", "dec"), route)

    order = sorted(range(dec_size), key=lambda j: (j % group, j // group))
    attends = functools.partial(attend, rep_size=rep_size, per_group=per_group, qpos=qpos, positions=positions)
    hops = [1] + list(range(rep_size - 1, 1, -1))
    own = {r: swap(kv, "rep", rep_size, r) for r in hops}
    for j in order[:2]:
        hand_over(j, near[-1])
    for j in order[2:3]:
        hand_over(j, near[-1], own[1], own[hops[1]])
    queries = rotate_queries(layer_queries, query_bias, cosine, sine)
    state = attends([((s, 0), near[s]) for s in range(pre_size)], queries=queries, state=None, last=False)
    far = []
    for r in hops[1:]:
        for s in range(1, pre_size):
            wait = (own[r], state[0]) if r == hops[1] else (own[r], arrived[order[0]])
            far.append(((s, r), swap(after(near[s], *wait), "rep", rep_size, r)))
    for j in order[3:]:
        hand_over(j, near[-1], state[0], own[hops[-1]])
    state = attends([((0, r), own[r]) for r in hops], queries=queries, state=state, last=False)
    for s in range(1, pre_size):
        far.append(((s, 1), swap(after(near[s], state[0], arrived[order[1]]), "rep", rep_size, 1)))
    state = attends(far, queries=queries, state=state, last=True)
    split = dec_size // 2
    arrange = functools.partial(place, (blk_count, capacity, hl, group), pre_size)
    got = [arrived[j] for j in order]
    decode_cache = arrange(order[:split], order, page_table, sends[0], got[:split], None)
    decode_cache = arrange(order[split:], [], page_table, sends[0], got[split:], decode_cache)
    return (state, decode_cache)


def solution(mesh):
    placed = (
        P(("pre", "rep"), "dec"),
        P(("pre", "rep"), None),
        P(("pre", "rep"), None),
        P("dec"),
        P(),
        P(),
        P(),
        P(),
        P(),
        P(),
        P("rep", "pre", "dec", None, None, None),
    )
    return jax.shard_map(
        shards,
        mesh=mesh,
        in_specs=placed,
        out_specs=(P(("pre", "rep"), "dec"), P("rep", "dec", None, "pre", None, None, None)),
        check_vma=False,
    )
```

```python
import functools

import jax
import jax.numpy as jnp
import numpy as np
from jax import lax
from jax.experimental import pallas as pl
from jax.experimental.pallas import tpu as pltpu
from jax.sharding import PartitionSpec as P

HEADS = 64
KVH = 8
HD = 128
BLOCK = 128

rope_base = 1000000.0
masked_score = -1e30
log2_e = 1.4426950408889634

ANY = pl.BlockSpec(memory_space=pl.ANY)
SMEM = pl.BlockSpec(memory_space=pltpu.SMEM)
VMEM = pl.BlockSpec(memory_space=pltpu.VMEM)
SMALL = pl.CostEstimate(flops=1, bytes_accessed=1, transcendentals=0)


def row_freqs():
    lane = np.arange(HD) % (HD // 2)
    freqs = 1.0 / rope_base ** (lane * (2.0 / HD))
    return jnp.asarray(freqs.astype(np.float32).reshape(1, HD))


def rotate(values, cosine, sine):
    return values * cosine + pltpu.roll(values, HD // 2, 1) * sine


def turn_kernel(
    dims,
    pos_ref,
    freq_ref,
    key_bias_ref,
    value_bias_ref,
    keys_hbm,
    values_hbm,
    kv_ref,
    cos_ref,
    sin_ref,
    qpos_ref,
    keys_buf,
    values_buf,
    sems,
):
    kv_local, head_count, rows, rep_size = dims
    pre, dec, rep = lax.axis_index("pre"), lax.axis_index("dec"), lax.axis_index("rep")
    kv_first = dec * head_count // (HEADS // KVH)
    columns = pl.ds(pl.multiple_of(kv_first * HD, HD), kv_local * HD)
    keys_in = pltpu.make_async_copy(keys_hbm.at[:, columns], keys_buf, sems.at[0])
    values_in = pltpu.make_async_copy(values_hbm.at[:, columns], values_buf, sems.at[1])
    keys_in.start()
    values_in.start()
    first = (pre * rep_size + rep) * (rows // HD)
    lanes = lax.broadcasted_iota(jnp.int32, (HD, HD), 1)
    for r in range(rows // HD):
        part = slice(r * HD, (r + 1) * HD)
        row = pos_ref[pl.ds(first + r, 1), :]
        column = jnp.broadcast_to(row, (HD, HD)).astype(jnp.float32).T
        qpos_ref[part, :] = column.astype(jnp.int32)
        angle = column * freq_ref[...]
        sine = jnp.sin(angle)
        cos_ref[part, :] = jnp.cos(angle)
        sin_ref[part, :] = jnp.where(lanes < HD // 2, -sine, sine)
    keys_in.wait()
    values_in.wait()
    for g in range(kv_local):
        where = pl.ds(pl.multiple_of((kv_first + g) * HD, HD), HD)
        part = slice(g * HD, (g + 1) * HD)
        shifted = keys_buf[:, part].astype(jnp.float32) + key_bias_ref[:, where]
        turned = rotate(shifted, cos_ref[...], sin_ref[...]).astype(jnp.bfloat16)
        biased = values_buf[:, part].astype(jnp.float32) + value_bias_ref[:, where]
        biased = biased.astype(jnp.bfloat16)
        kv_ref[0, g] = turned
        kv_ref[1, g] = biased


def turn(dims, positions, key_bias, value_bias, keys, values):
    kv_local, head_count, rows, rep_size = dims
    return pl.pallas_call(
        functools.partial(turn_kernel, dims),
        out_shape=[
            jax.ShapeDtypeStruct((2, kv_local, rows, HD), jnp.bfloat16),
            jax.ShapeDtypeStruct((rows, HD), jnp.float32),
            jax.ShapeDtypeStruct((rows, HD), jnp.float32),
            jax.ShapeDtypeStruct((rows, HD), jnp.int32),
        ],
        in_specs=[VMEM] * 4 + [ANY] * 2,
        out_specs=[VMEM] * 4,
        scratch_shapes=[
            pltpu.VMEM((rows, kv_local * HD), jnp.bfloat16),
            pltpu.VMEM((rows, kv_local * HD), jnp.bfloat16),
            pltpu.SemaphoreType.DMA((2,)),
        ],
        cost_estimate=SMALL,
        name="turn",
    )(
        positions.reshape(-1, HD),
        row_freqs(),
        key_bias.reshape(1, -1),
        value_bias.reshape(1, -1),
        keys,
        values,
    )


def pack_kernel(dims, page_ref, lengths_ref, replica_ref, kv_hbm, cache_hbm, *rest):
    blk_count, group, dec_size = dims
    sends = rest[:dec_size]
    held, valid, counts, in_sems, out_sems = rest[dec_size:]
    pre, dec, rep = lax.axis_index("pre"), lax.axis_index("dec"), lax.axis_index("rep")
    blocks_in = [
        pltpu.make_async_copy(cache_hbm.at[0, b], held.at[b], in_sems.at[b])
        for b in range(blk_count)
    ]
    for copy in blocks_in:
        copy.start()
    blocks_all = valid.shape[0]
    for k in range(blocks_all):
        valid[k] = 0
    for d in range(dec_size):
        counts[d] = 0

    def request(i, start):
        mine = replica_ref[i] == rep
        length = lengths_ref[i]
        number = jnp.where(mine, (length + (BLOCK - 1)) // BLOCK, 0)

        def block(k, carry):
            valid[start + k] = jnp.minimum(BLOCK, length - BLOCK * k)
            return carry

        lax.fori_loop(0, jnp.minimum(number, blocks_all - start), block, 0)
        return start + number

    lax.fori_loop(0, lengths_ref.shape[0], request, 0)
    place = pre * group + dec % group
    lane = lax.broadcasted_iota(jnp.int32, held.shape[1:], len(held.shape) - 2)
    for b in range(blk_count):
        k = pre * blk_count + b
        blocks_in[b].wait()
        limit = valid[k]

        @pl.when(limit < BLOCK)
        def _(b=b, limit=limit):
            held[b] = jnp.where(lane < limit, held[b], jnp.zeros_like(held[b]))

        target = page_ref[rep, k]
        rank = counts[target]
        counts[target] = rank + 1
        for j in range(dec_size):

            @pl.when(target == (place ^ j))
            def _(b=b, j=j, rank=rank):
                pltpu.make_async_copy(held.at[b], sends[j].at[rank], out_sems.at[b]).start()

    for b in range(blk_count):
        pltpu.make_async_copy(held.at[b], sends[0].at[0], out_sems.at[b]).wait()


def pack(dims, capacity, page_table, lengths, replica_of, kv, cache):
    blk_count, group, dec_size = dims
    block = cache.shape[2:]
    return pl.pallas_call(
        functools.partial(pack_kernel, dims),
        out_shape=[jax.ShapeDtypeStruct((capacity,) + block, jnp.bfloat16)] * dec_size,
        in_specs=[SMEM] * 3 + [ANY] * 2,
        out_specs=[ANY] * dec_size,
        scratch_shapes=[
            pltpu.VMEM((blk_count,) + block, jnp.bfloat16),
            pltpu.SMEM((page_table.shape[1],), jnp.int32),
            pltpu.SMEM((dec_size,), jnp.int32),
            pltpu.SemaphoreType.DMA((blk_count,)),
            pltpu.SemaphoreType.DMA((blk_count,)),
        ],
        cost_estimate=SMALL,
        name="pack",
    )(page_table, lengths, replica_of, kv, cache)


def after(value, *before):
    return lax.optimization_barrier((value,) + before)[0] if before else value


def query_kernel(query_ref, bias_ref, cos_ref, sin_ref, out_ref):
    for h in range(out_ref.shape[0]):
        columns = slice(h * HD, (h + 1) * HD)
        shifted = query_ref[:, columns].astype(jnp.float32) + bias_ref[:, columns]
        out_ref[h] = rotate(shifted, cos_ref[...], sin_ref[...]).astype(jnp.bfloat16)


def rotate_queries(queries, bias, cosine, sine):
    rows, columns = queries.shape
    return pl.pallas_call(
        query_kernel,
        out_shape=jax.ShapeDtypeStruct((columns // HD, rows, HD), jnp.bfloat16),
        in_specs=[VMEM] * 4,
        out_specs=VMEM,
        cost_estimate=SMALL,
        name="rotate_queries",
    )(queries, bias.reshape(1, -1), cosine, sine)


def attend_kernel(moves, rep_size, first, last, query_ref, qpos_ref, pos_ref, *rest):
    chunks, rest = rest[: len(moves)], rest[len(moves) :]
    if not first:
        stat_in, sum_in, rest = rest[0], rest[1], rest[2:]
    outs = rest
    step_heads, rows, _ = query_ref.shape
    half = HD // 2
    pre, rep = lax.axis_index("pre"), lax.axis_index("rep")
    scale = HD ** (-0.5) * log2_e
    qpos = qpos_ref[:, :1]
    lanes = lax.broadcasted_iota(jnp.int32, (rows, HD), 1)
    bias, keys, values = [], [], []
    for (move_pre, move_rep), chunk in zip(moves, chunks):
        block = (pre ^ move_pre) * rep_size + (rep ^ move_rep)
        parts = [pos_ref[pl.ds(block * (rows // HD) + r, 1), :] for r in range(rows // HD)]
        bias.append(jnp.concatenate(parts, axis=1) <= qpos)
        keys.append(chunk[0, 0])
        values.append(jnp.concatenate([chunk[1, 0], jnp.ones((rows, HD), jnp.bfloat16)], axis=1))
    stat = jnp.zeros((rows, HD), jnp.float32)
    for h in range(step_heads):
        query = query_ref[h]
        scores = []
        for allowed, key in zip(bias, keys):
            product = lax.dot_general(
                query, key, (((1,), (1,)), ((), ())), preferred_element_type=jnp.float32
            )
            scores.append(jnp.where(allowed, product, masked_score))
        newest = jnp.max(functools.reduce(jnp.maximum, scores), axis=1, keepdims=True)
        if not first:
            best = stat_in[0, :, h : h + 1]
            newest = jnp.maximum(newest, best)
            decay = jnp.exp2((best - newest) * scale)
        both = 0.0
        for score, value in zip(scores, values):
            weights = jnp.exp2((score - newest) * scale)
            both = both + jnp.dot(
                weights.astype(jnp.bfloat16), value, preferred_element_type=jnp.float32
            )
        added, total = both[:, :HD], both[:, HD:]
        if not first:
            total = total + stat_in[0, :, half + h : half + h + 1] * decay
            added = added + sum_in[h] * decay
        if last:
            outs[0][:, h * HD : (h + 1) * HD] = (added / total).astype(jnp.bfloat16)
        else:
            stat = jnp.where(lanes == h, newest, jnp.where(lanes == half + h, total, stat))
            outs[1][h] = added
    if not last:
        outs[0][0] = stat


def attend(pairs, rep_size, per_group, queries, qpos, positions, state, last):
    heads, rows, _ = queries.shape
    step_heads = per_group
    first = state is None
    moves, chunks = zip(*pairs)
    whole = lambda i: (0, 0)
    by_head = pl.BlockSpec((step_heads, rows, HD), lambda i: (i, 0, 0))
    by_step = pl.BlockSpec((1, rows, HD), lambda i: (i, 0, 0))
    chunk_spec = pl.BlockSpec((2, 1, rows, HD), lambda i: (0, i, 0, 0))
    pos2 = positions.reshape(-1, HD)
    in_specs = (
        [by_head, pl.BlockSpec((rows, HD), whole), pl.BlockSpec(pos2.shape, whole)]
        + [chunk_spec] * len(chunks)
        + ([] if first else [by_step, by_head])
    )
    if last:
        out_shape = jax.ShapeDtypeStruct((rows, heads * HD), jnp.bfloat16)
        out_specs = pl.BlockSpec((rows, step_heads * HD), lambda i: (0, i))
    else:
        out_shape = [
            jax.ShapeDtypeStruct((heads // step_heads, rows, HD), jnp.float32),
            jax.ShapeDtypeStruct((heads, rows, HD), jnp.float32),
        ]
        out_specs = [by_step, by_head]
    return pl.pallas_call(
        functools.partial(attend_kernel, moves, rep_size, first, last),
        grid=(heads // step_heads,),
        out_shape=out_shape,
        in_specs=in_specs,
        out_specs=out_specs,
        compiler_params=pltpu.CompilerParams(vmem_limit_bytes=40 << 20),
        cost_estimate=SMALL,
        name="attend",
    )(queries, qpos, pos2, *chunks, *(() if first else state))


def place_kernel(dims, here, rest_j, page_ref, own_hbm, *rest):
    blk_count, capacity, hl, group = dims
    arrived, rest = rest[: len(here)], rest[len(here) :]
    out_hbm, held, zeros, in_sems, out_sems = rest[-5:]
    pre, dec, rep = lax.axis_index("pre"), lax.axis_index("dec"), lax.axis_index("rep")

    def goal(j):
        source = dec ^ j
        run, part = source // group, source % group
        used = functools.reduce(
            jnp.logical_or,
            [page_ref[rep, run * blk_count + b] == dec for b in range(blk_count)],
        )
        return used, lambda c: out_hbm.at[0, 0, run * capacity + c, pl.ds(part * hl, hl)]

    moves = []
    for n, j in enumerate(here):
        used, to = goal(j)
        for c in range(capacity):
            inward = pltpu.make_async_copy(arrived[n].at[c], held.at[n, c], in_sems.at[n, c])
            outward = pltpu.make_async_copy(held.at[n, c], to(c), out_sems.at[n, c])
            moves.append((used, inward, outward))
            local = used & (dec // group == pre) if j == 0 else None
            if j == 0:
                kept = pltpu.make_async_copy(own_hbm.at[c], held.at[n, c], in_sems.at[n, c])

                @pl.when(local)
                def _(kept=kept):
                    kept.start()

            @pl.when(used if local is None else used & jnp.logical_not(local))
            def _(inward=inward):
                inward.start()

    fills = []
    if rest_j:
        zeros[...] = jnp.zeros_like(zeros)
        for n, j in enumerate(rest_j):
            used, to = goal(j)
            for c in range(capacity):
                fill = pltpu.make_async_copy(zeros, to(c), out_sems.at[len(here) + n, c])
                fills.append((used, fill))

                @pl.when(jnp.logical_not(used))
                def _(fill=fill):
                    fill.start()

    for used, inward, outward in moves:

        @pl.when(used)
        def _(inward=inward, outward=outward):
            inward.wait()
            outward.start()

    for used, inward, outward in moves:

        @pl.when(used)
        def _(outward=outward):
            outward.wait()

    for used, fill in fills:

        @pl.when(jnp.logical_not(used))
        def _(fill=fill):
            fill.wait()


def place(dims, pre_size, here, rest_j, page_table, own, arrived, buffer):
    blk_count, capacity, hl, group = dims
    block = arrived[0].shape[2:]
    count = len(here)
    kept = [] if buffer is None else [buffer]
    return pl.pallas_call(
        functools.partial(place_kernel, dims, here, rest_j),
        out_shape=jax.ShapeDtypeStruct((1, 1, pre_size * capacity, group * hl) + block, jnp.bfloat16),
        in_specs=[SMEM] + [ANY] * (1 + count + len(kept)),
        out_specs=ANY,
        scratch_shapes=[
            pltpu.VMEM((count, capacity, hl) + block, jnp.bfloat16),
            pltpu.VMEM((hl,) + block, jnp.bfloat16),
            pltpu.SemaphoreType.DMA((count, capacity)),
            pltpu.SemaphoreType.DMA((count + len(rest_j), capacity)),
        ],
        input_output_aliases={2 + count: 0} if kept else {},
        cost_estimate=SMALL,
        name="place",
    )(page_table, own, *arrived, *kept)


def shards(
    layer_queries,
    layer_keys,
    layer_values,
    query_bias,
    key_bias,
    value_bias,
    positions,
    lengths,
    replica_of,
    page_table,
    prefill_cache,
):
    pre_size, dec_size, rep_size = (lax.axis_size(a) for a in ("pre", "dec", "rep"))
    rows = layer_queries.shape[0]
    head_count = layer_queries.shape[1] // HD
    group_size = HEADS // KVH
    kv_local = max(1, head_count // group_size)
    per_group = head_count // kv_local
    blk_count, hl = prefill_cache.shape[1], prefill_cache.shape[2]
    capacity = 2 * blk_count // dec_size
    group = dec_size // pre_size
    kv, cosine, sine, qpos = turn(
        (kv_local, head_count, rows, rep_size), positions, key_bias, value_bias,
        layer_keys, layer_values,
    )
    sends = pack((blk_count, group, dec_size), capacity, page_table, lengths, replica_of, kv, prefill_cache)
    swap = lambda value, axis, size, hop: lax.ppermute(
        value, axis, [(i, i ^ hop) for i in range(size)]
    )
    near = [kv] + [swap(kv, "pre", pre_size, s) for s in range(1, pre_size)]
    arrived = {}

    def hand_over(j, *before):
        route = []
        for p in range(pre_size):
            for d in range(dec_size):
                goal = (p * group + d % group) ^ j
                pair = (p * dec_size + d, (d // group) * dec_size + goal)
                if pair[0] != pair[1]:
                    route.append(pair)
        arrived[j] = lax.ppermute(after(sends[j], *before), ("pre", "dec"), route)

    order = sorted(range(dec_size), key=lambda j: (j % group, j // group))
    attends = functools.partial(attend, rep_size=rep_size, per_group=per_group, qpos=qpos, positions=positions)
    hops = [1] + list(range(rep_size - 1, 1, -1))
    own = {r: swap(kv, "rep", rep_size, r) for r in hops}
    for j in order[:2]:
        hand_over(j, near[-1])
    for j in order[2:3]:
        hand_over(j, near[-1], own[hops[1]], own[hops[-1]])
    queries = rotate_queries(layer_queries, query_bias, cosine, sine)
    state = attends([((s, 0), near[s]) for s in range(pre_size)], queries=queries, state=None, last=False)
    far = []
    for r in hops[1:]:
        for s in range(1, pre_size):
            wait = (own[r], state[0]) if r == hops[1] else (own[r], arrived[order[0]])
            far.append(((s, r), swap(after(near[s], *wait), "rep", rep_size, r)))
    for j in order[3:]:
        hand_over(j, near[-1], state[0], own[1])
    for s in range(1, pre_size):
        far.append(((s, 1), swap(after(near[s], own[1], arrived[order[1]]), "rep", rep_size, 1)))
    ready = (after(state[0], arrived[order[0]], arrived[order[1]]), state[1])
    state = attends([((0, r), own[r]) for r in hops], queries=queries, state=ready, last=False)
    state = attends(far, queries=queries, state=state, last=True)
    split = dec_size // 2
    arrange = functools.partial(place, (blk_count, capacity, hl, group), pre_size)
    got = [arrived[j] for j in order]
    decode_cache = arrange(order[:split], order, page_table, sends[0], got[:split], None)
    decode_cache = arrange(
        order[split:], [], page_table, sends[0], got[split:], after(decode_cache, state)
    )
    return (state, decode_cache)


def solution(mesh):
    placed = (
        P(("pre", "rep"), "dec"),
        P(("pre", "rep"), None),
        P(("pre", "rep"), None),
        P("dec"),
        P(),
        P(),
        P(),
        P(),
        P(),
        P(),
        P("rep", "pre", "dec", None, None, None),
    )
    return jax.shard_map(
        shards,
        mesh=mesh,
        in_specs=placed,
        out_specs=(P(("pre", "rep"), "dec"), P("rep", "dec", None, "pre", None, None, None)),
        check_vma=False,
    )
```

```python
import functools

import jax
import jax.numpy as jnp
import numpy as np
from jax import lax
from jax.experimental import pallas as pl
from jax.experimental.pallas import tpu as pltpu
from jax.sharding import PartitionSpec as P

HEADS = 64
KVH = 8
HD = 128
BLOCK = 128

rope_base = 1000000.0
masked_score = -1e30
log2_e = 1.4426950408889634

ANY = pl.BlockSpec(memory_space=pl.ANY)
SMEM = pl.BlockSpec(memory_space=pltpu.SMEM)
VMEM = pl.BlockSpec(memory_space=pltpu.VMEM)
SMALL = pl.CostEstimate(flops=1, bytes_accessed=1, transcendentals=0)


def row_freqs():
    lane = np.arange(HD) % (HD // 2)
    freqs = 1.0 / rope_base ** (lane * (2.0 / HD))
    return jnp.asarray(freqs.astype(np.float32).reshape(1, HD))


def rotate(values, cosine, sine):
    return values * cosine + pltpu.roll(values, HD // 2, 1) * sine


def turn_kernel(
    dims,
    pos_ref,
    freq_ref,
    key_bias_ref,
    value_bias_ref,
    keys_hbm,
    values_hbm,
    kv_ref,
    cos_ref,
    sin_ref,
    qpos_ref,
    keys_buf,
    values_buf,
    sems,
):
    kv_local, head_count, rows, rep_size = dims
    pre, dec, rep = lax.axis_index("pre"), lax.axis_index("dec"), lax.axis_index("rep")
    kv_first = dec * head_count // (HEADS // KVH)
    columns = pl.ds(pl.multiple_of(kv_first * HD, HD), kv_local * HD)
    keys_in = pltpu.make_async_copy(keys_hbm.at[:, columns], keys_buf, sems.at[0])
    values_in = pltpu.make_async_copy(values_hbm.at[:, columns], values_buf, sems.at[1])
    keys_in.start()
    values_in.start()
    first = (pre * rep_size + rep) * (rows // HD)
    lanes = lax.broadcasted_iota(jnp.int32, (HD, HD), 1)
    for r in range(rows // HD):
        part = slice(r * HD, (r + 1) * HD)
        row = pos_ref[pl.ds(first + r, 1), :]
        column = jnp.broadcast_to(row, (HD, HD)).astype(jnp.float32).T
        qpos_ref[part, :] = column.astype(jnp.int32)
        angle = column * freq_ref[...]
        sine = jnp.sin(angle)
        cos_ref[part, :] = jnp.cos(angle)
        sin_ref[part, :] = jnp.where(lanes < HD // 2, -sine, sine)
    keys_in.wait()
    values_in.wait()
    for g in range(kv_local):
        where = pl.ds(pl.multiple_of((kv_first + g) * HD, HD), HD)
        part = slice(g * HD, (g + 1) * HD)
        shifted = keys_buf[:, part].astype(jnp.float32) + key_bias_ref[:, where]
        turned = rotate(shifted, cos_ref[...], sin_ref[...]).astype(jnp.bfloat16)
        biased = values_buf[:, part].astype(jnp.float32) + value_bias_ref[:, where]
        biased = biased.astype(jnp.bfloat16)
        kv_ref[0, g] = turned
        kv_ref[1, g] = biased


def turn(dims, positions, key_bias, value_bias, keys, values):
    kv_local, head_count, rows, rep_size = dims
    return pl.pallas_call(
        functools.partial(turn_kernel, dims),
        out_shape=[
            jax.ShapeDtypeStruct((2, kv_local, rows, HD), jnp.bfloat16),
            jax.ShapeDtypeStruct((rows, HD), jnp.float32),
            jax.ShapeDtypeStruct((rows, HD), jnp.float32),
            jax.ShapeDtypeStruct((rows, HD), jnp.int32),
        ],
        in_specs=[VMEM] * 4 + [ANY] * 2,
        out_specs=[VMEM] * 4,
        scratch_shapes=[
            pltpu.VMEM((rows, kv_local * HD), jnp.bfloat16),
            pltpu.VMEM((rows, kv_local * HD), jnp.bfloat16),
            pltpu.SemaphoreType.DMA((2,)),
        ],
        cost_estimate=SMALL,
        name="turn",
    )(
        positions.reshape(-1, HD),
        row_freqs(),
        key_bias.reshape(1, -1),
        value_bias.reshape(1, -1),
        keys,
        values,
    )


def pack_kernel(dims, page_ref, lengths_ref, replica_ref, kv_hbm, cache_hbm, *rest):
    blk_count, group, dec_size = dims
    sends = rest[:dec_size]
    held, valid, counts, in_sems, out_sems = rest[dec_size:]
    pre, dec, rep = lax.axis_index("pre"), lax.axis_index("dec"), lax.axis_index("rep")
    blocks_in = [
        pltpu.make_async_copy(cache_hbm.at[0, b], held.at[b], in_sems.at[b])
        for b in range(blk_count)
    ]
    for copy in blocks_in:
        copy.start()
    blocks_all = valid.shape[0]
    for k in range(blocks_all):
        valid[k] = 0
    for d in range(dec_size):
        counts[d] = 0

    def request(i, start):
        mine = replica_ref[i] == rep
        length = lengths_ref[i]
        number = jnp.where(mine, (length + (BLOCK - 1)) // BLOCK, 0)

        def block(k, carry):
            valid[start + k] = jnp.minimum(BLOCK, length - BLOCK * k)
            return carry

        lax.fori_loop(0, jnp.minimum(number, blocks_all - start), block, 0)
        return start + number

    lax.fori_loop(0, lengths_ref.shape[0], request, 0)
    place = pre * group + dec % group
    lane = lax.broadcasted_iota(jnp.int32, held.shape[1:], len(held.shape) - 2)
    for b in range(blk_count):
        k = pre * blk_count + b
        blocks_in[b].wait()
        limit = valid[k]

        @pl.when(limit < BLOCK)
        def _(b=b, limit=limit):
            held[b] = jnp.where(lane < limit, held[b], jnp.zeros_like(held[b]))

        target = page_ref[rep, k]
        rank = counts[target]
        counts[target] = rank + 1
        for j in range(dec_size):

            @pl.when(target == (place ^ j))
            def _(b=b, j=j, rank=rank):
                pltpu.make_async_copy(held.at[b], sends[j].at[rank], out_sems.at[b]).start()

    for b in range(blk_count):
        pltpu.make_async_copy(held.at[b], sends[0].at[0], out_sems.at[b]).wait()


def pack(dims, capacity, page_table, lengths, replica_of, kv, cache):
    blk_count, group, dec_size = dims
    block = cache.shape[2:]
    return pl.pallas_call(
        functools.partial(pack_kernel, dims),
        out_shape=[jax.ShapeDtypeStruct((capacity,) + block, jnp.bfloat16)] * dec_size,
        in_specs=[SMEM] * 3 + [ANY] * 2,
        out_specs=[ANY] * dec_size,
        scratch_shapes=[
            pltpu.VMEM((blk_count,) + block, jnp.bfloat16),
            pltpu.SMEM((page_table.shape[1],), jnp.int32),
            pltpu.SMEM((dec_size,), jnp.int32),
            pltpu.SemaphoreType.DMA((blk_count,)),
            pltpu.SemaphoreType.DMA((blk_count,)),
        ],
        cost_estimate=SMALL,
        name="pack",
    )(page_table, lengths, replica_of, kv, cache)


def after(value, *before):
    return lax.optimization_barrier((value,) + before)[0] if before else value


def query_kernel(query_ref, bias_ref, cos_ref, sin_ref, out_ref):
    for h in range(out_ref.shape[0]):
        columns = slice(h * HD, (h + 1) * HD)
        shifted = query_ref[:, columns].astype(jnp.float32) + bias_ref[:, columns]
        out_ref[h] = rotate(shifted, cos_ref[...], sin_ref[...]).astype(jnp.bfloat16)


def rotate_queries(queries, bias, cosine, sine):
    rows, columns = queries.shape
    return pl.pallas_call(
        query_kernel,
        out_shape=jax.ShapeDtypeStruct((columns // HD, rows, HD), jnp.bfloat16),
        in_specs=[VMEM] * 4,
        out_specs=VMEM,
        cost_estimate=SMALL,
        name="rotate_queries",
    )(queries, bias.reshape(1, -1), cosine, sine)


def attend_kernel(moves, rep_size, first, last, query_ref, qpos_ref, pos_ref, *rest):
    chunks, rest = rest[: len(moves)], rest[len(moves) :]
    if not first:
        stat_in, sum_in, rest = rest[0], rest[1], rest[2:]
    outs = rest
    step_heads, rows, _ = query_ref.shape
    half = HD // 2
    pre, rep = lax.axis_index("pre"), lax.axis_index("rep")
    scale = HD ** (-0.5) * log2_e
    qpos = qpos_ref[:, :1]
    lanes = lax.broadcasted_iota(jnp.int32, (rows, HD), 1)
    bias, keys, values = [], [], []
    for (move_pre, move_rep), chunk in zip(moves, chunks):
        block = (pre ^ move_pre) * rep_size + (rep ^ move_rep)
        parts = [pos_ref[pl.ds(block * (rows // HD) + r, 1), :] for r in range(rows // HD)]
        bias.append(jnp.concatenate(parts, axis=1) <= qpos)
        keys.append(chunk[0, 0])
        values.append(jnp.concatenate([chunk[1, 0], jnp.ones((rows, HD), jnp.bfloat16)], axis=1))
    stat = jnp.zeros((rows, HD), jnp.float32)
    for h in range(step_heads):
        query = query_ref[h]
        scores = []
        for allowed, key in zip(bias, keys):
            product = lax.dot_general(
                query, key, (((1,), (1,)), ((), ())), preferred_element_type=jnp.float32
            )
            scores.append(jnp.where(allowed, product, masked_score))
        newest = jnp.max(functools.reduce(jnp.maximum, scores), axis=1, keepdims=True)
        if not first:
            best = stat_in[0, :, h : h + 1]
            newest = jnp.maximum(newest, best)
            decay = jnp.exp2((best - newest) * scale)
        both = 0.0
        for score, value in zip(scores, values):
            weights = jnp.exp2((score - newest) * scale)
            both = both + jnp.dot(
                weights.astype(jnp.bfloat16), value, preferred_element_type=jnp.float32
            )
        added, total = both[:, :HD], both[:, HD:]
        if not first:
            total = total + stat_in[0, :, half + h : half + h + 1] * decay
            added = added + sum_in[h] * decay
        if last:
            outs[0][:, h * HD : (h + 1) * HD] = (added / total).astype(jnp.bfloat16)
        else:
            stat = jnp.where(lanes == h, newest, jnp.where(lanes == half + h, total, stat))
            outs[1][h] = added
    if not last:
        outs[0][0] = stat


def attend(pairs, rep_size, per_group, queries, qpos, positions, state, last):
    heads, rows, _ = queries.shape
    step_heads = per_group
    first = state is None
    moves, chunks = zip(*pairs)
    whole = lambda i: (0, 0)
    by_head = pl.BlockSpec((step_heads, rows, HD), lambda i: (i, 0, 0))
    by_step = pl.BlockSpec((1, rows, HD), lambda i: (i, 0, 0))
    chunk_spec = pl.BlockSpec((2, 1, rows, HD), lambda i: (0, i, 0, 0))
    pos2 = positions.reshape(-1, HD)
    in_specs = (
        [by_head, pl.BlockSpec((rows, HD), whole), pl.BlockSpec(pos2.shape, whole)]
        + [chunk_spec] * len(chunks)
        + ([] if first else [by_step, by_head])
    )
    if last:
        out_shape = jax.ShapeDtypeStruct((rows, heads * HD), jnp.bfloat16)
        out_specs = pl.BlockSpec((rows, step_heads * HD), lambda i: (0, i))
    else:
        out_shape = [
            jax.ShapeDtypeStruct((heads // step_heads, rows, HD), jnp.float32),
            jax.ShapeDtypeStruct((heads, rows, HD), jnp.float32),
        ]
        out_specs = [by_step, by_head]
    return pl.pallas_call(
        functools.partial(attend_kernel, moves, rep_size, first, last),
        grid=(heads // step_heads,),
        out_shape=out_shape,
        in_specs=in_specs,
        out_specs=out_specs,
        compiler_params=pltpu.CompilerParams(vmem_limit_bytes=40 << 20),
        cost_estimate=SMALL,
        name="attend",
    )(queries, qpos, pos2, *chunks, *(() if first else state))


def place_kernel(dims, here, rest_j, page_ref, own_hbm, *rest):
    blk_count, capacity, hl, group = dims
    arrived, rest = rest[: len(here)], rest[len(here) :]
    out_hbm, held, zeros, in_sems, out_sems = rest[-5:]
    pre, dec, rep = lax.axis_index("pre"), lax.axis_index("dec"), lax.axis_index("rep")

    def goal(j):
        source = dec ^ j
        run, part = source // group, source % group
        used = functools.reduce(
            jnp.logical_or,
            [page_ref[rep, run * blk_count + b] == dec for b in range(blk_count)],
        )
        return used, lambda c: out_hbm.at[0, 0, run * capacity + c, pl.ds(part * hl, hl)]

    moves = []
    for n, j in enumerate(here):
        used, to = goal(j)
        for c in range(capacity):
            inward = pltpu.make_async_copy(arrived[n].at[c], held.at[n, c], in_sems.at[n, c])
            outward = pltpu.make_async_copy(held.at[n, c], to(c), out_sems.at[n, c])
            moves.append((used, inward, outward))
            local = used & (dec // group == pre) if j == 0 else None
            if j == 0:
                kept = pltpu.make_async_copy(own_hbm.at[c], held.at[n, c], in_sems.at[n, c])

                @pl.when(local)
                def _(kept=kept):
                    kept.start()

            @pl.when(used if local is None else used & jnp.logical_not(local))
            def _(inward=inward):
                inward.start()

    fills = []
    if rest_j:
        zeros[...] = jnp.zeros_like(zeros)
        for n, j in enumerate(rest_j):
            used, to = goal(j)
            for c in range(capacity):
                fill = pltpu.make_async_copy(zeros, to(c), out_sems.at[len(here) + n, c])
                fills.append((used, fill))

                @pl.when(jnp.logical_not(used))
                def _(fill=fill):
                    fill.start()

    for used, inward, outward in moves:

        @pl.when(used)
        def _(inward=inward, outward=outward):
            inward.wait()
            outward.start()

    for used, inward, outward in moves:

        @pl.when(used)
        def _(outward=outward):
            outward.wait()

    for used, fill in fills:

        @pl.when(jnp.logical_not(used))
        def _(fill=fill):
            fill.wait()


def place(dims, pre_size, here, rest_j, page_table, own, arrived, buffer):
    blk_count, capacity, hl, group = dims
    block = arrived[0].shape[2:]
    count = len(here)
    kept = [] if buffer is None else [buffer]
    return pl.pallas_call(
        functools.partial(place_kernel, dims, here, rest_j),
        out_shape=jax.ShapeDtypeStruct((1, 1, pre_size * capacity, group * hl) + block, jnp.bfloat16),
        in_specs=[SMEM] + [ANY] * (1 + count + len(kept)),
        out_specs=ANY,
        scratch_shapes=[
            pltpu.VMEM((count, capacity, hl) + block, jnp.bfloat16),
            pltpu.VMEM((hl,) + block, jnp.bfloat16),
            pltpu.SemaphoreType.DMA((count, capacity)),
            pltpu.SemaphoreType.DMA((count + len(rest_j), capacity)),
        ],
        input_output_aliases={2 + count: 0} if kept else {},
        cost_estimate=SMALL,
        name="place",
    )(page_table, own, *arrived, *kept)


def shards(
    layer_queries,
    layer_keys,
    layer_values,
    query_bias,
    key_bias,
    value_bias,
    positions,
    lengths,
    replica_of,
    page_table,
    prefill_cache,
):
    pre_size, dec_size, rep_size = (lax.axis_size(a) for a in ("pre", "dec", "rep"))
    rows = layer_queries.shape[0]
    head_count = layer_queries.shape[1] // HD
    group_size = HEADS // KVH
    kv_local = max(1, head_count // group_size)
    per_group = head_count // kv_local
    blk_count, hl = prefill_cache.shape[1], prefill_cache.shape[2]
    capacity = 2 * blk_count // dec_size
    group = dec_size // pre_size
    kv, cosine, sine, qpos = turn(
        (kv_local, head_count, rows, rep_size), positions, key_bias, value_bias,
        layer_keys, layer_values,
    )
    sends = pack((blk_count, group, dec_size), capacity, page_table, lengths, replica_of, kv, prefill_cache)
    swap = lambda value, axis, size, hop: lax.ppermute(
        value, axis, [(i, i ^ hop) for i in range(size)]
    )
    near = [kv] + [swap(kv, "pre", pre_size, s) for s in range(1, pre_size)]
    arrived = {}

    def hand_over(j, *before):
        route = []
        for p in range(pre_size):
            for d in range(dec_size):
                goal = (p * group + d % group) ^ j
                pair = (p * dec_size + d, (d // group) * dec_size + goal)
                if pair[0] != pair[1]:
                    route.append(pair)
        arrived[j] = lax.ppermute(after(sends[j], *before), ("pre", "dec"), route)

    order = sorted(range(dec_size), key=lambda j: (j % group, j // group))
    attends = functools.partial(attend, rep_size=rep_size, per_group=per_group, qpos=qpos, positions=positions)
    hops = [1] + list(range(rep_size - 1, 1, -1))
    own = {r: swap(kv, "rep", rep_size, r) for r in hops}
    for j in order[:2]:
        hand_over(j, near[-1])
    for j in order[2:3]:
        hand_over(j, near[-1], own[hops[1]], own[hops[-1]], own[1])
    queries = rotate_queries(layer_queries, query_bias, cosine, sine)
    state = attends([((s, 0), near[s]) for s in range(pre_size)], queries=queries, state=None, last=False)
    far = []
    for r in hops[1:]:
        for s in range(1, pre_size):
            wait = (own[r], state[0]) if r == hops[1] else (own[r], arrived[order[0]])
            far.append(((s, r), swap(after(near[s], *wait), "rep", rep_size, r)))
    for j in order[3:]:
        hand_over(j, near[-1], state[0], own[1], own[hops[-1]])
    for s in range(1, pre_size):
        far.append(((s, 1), swap(after(near[s], own[1], arrived[order[1]]), "rep", rep_size, 1)))
    ready = (after(state[0], arrived[order[0]], arrived[order[1]]), state[1])
    state = attends([((0, r), own[r]) for r in hops], queries=queries, state=ready, last=False)
    state = attends(far, queries=queries, state=state, last=True)
    split = dec_size // 2
    arrange = functools.partial(place, (blk_count, capacity, hl, group), pre_size)
    got = [arrived[j] for j in order]
    decode_cache = arrange(order[:split], order, page_table, sends[0], got[:split], None)
    decode_cache = arrange(
        order[split:], [], page_table, sends[0], got[split:], after(decode_cache, state)
    )
    return (state, decode_cache)


def solution(mesh):
    placed = (
        P(("pre", "rep"), "dec"),
        P(("pre", "rep"), None),
        P(("pre", "rep"), None),
        P("dec"),
        P(),
        P(),
        P(),
        P(),
        P(),
        P(),
        P("rep", "pre", "dec", None, None, None),
    )
    return jax.shard_map(
        shards,
        mesh=mesh,
        in_specs=placed,
        out_specs=(P(("pre", "rep"), "dec"), P("rep", "dec", None, "pre", None, None, None)),
        check_vma=False,
    )
```

```python
import functools

import jax
import jax.numpy as jnp
import numpy as np
from jax import lax
from jax.experimental import pallas as pl
from jax.experimental.pallas import tpu as pltpu
from jax.sharding import PartitionSpec as P

HEADS = 64
KVH = 8
HD = 128
BLOCK = 128

rope_base = 1000000.0
masked_score = -1e30
log2_e = 1.4426950408889634

ANY = pl.BlockSpec(memory_space=pl.ANY)
SMEM = pl.BlockSpec(memory_space=pltpu.SMEM)
VMEM = pl.BlockSpec(memory_space=pltpu.VMEM)
SMALL = pl.CostEstimate(flops=1, bytes_accessed=1, transcendentals=0)


def row_freqs():
    lane = np.arange(HD) % (HD // 2)
    freqs = 1.0 / rope_base ** (lane * (2.0 / HD))
    return jnp.asarray(freqs.astype(np.float32).reshape(1, HD))


def rotate(values, cosine, sine):
    return values * cosine + pltpu.roll(values, HD // 2, 1) * sine


def turn_kernel(
    dims,
    pos_ref,
    freq_ref,
    key_bias_ref,
    value_bias_ref,
    keys_hbm,
    values_hbm,
    kv_ref,
    cos_ref,
    sin_ref,
    qpos_ref,
    keys_buf,
    values_buf,
    sems,
):
    kv_local, head_count, rows, rep_size = dims
    pre, dec, rep = lax.axis_index("pre"), lax.axis_index("dec"), lax.axis_index("rep")
    kv_first = dec * head_count // (HEADS // KVH)
    columns = pl.ds(pl.multiple_of(kv_first * HD, HD), kv_local * HD)
    keys_in = pltpu.make_async_copy(keys_hbm.at[:, columns], keys_buf, sems.at[0])
    values_in = pltpu.make_async_copy(values_hbm.at[:, columns], values_buf, sems.at[1])
    keys_in.start()
    values_in.start()
    first = (pre * rep_size + rep) * (rows // HD)
    lanes = lax.broadcasted_iota(jnp.int32, (HD, HD), 1)
    for r in range(rows // HD):
        part = slice(r * HD, (r + 1) * HD)
        row = pos_ref[pl.ds(first + r, 1), :]
        column = jnp.broadcast_to(row, (HD, HD)).astype(jnp.float32).T
        qpos_ref[part, :] = column.astype(jnp.int32)
        angle = column * freq_ref[...]
        sine = jnp.sin(angle)
        cos_ref[part, :] = jnp.cos(angle)
        sin_ref[part, :] = jnp.where(lanes < HD // 2, -sine, sine)
    keys_in.wait()
    values_in.wait()
    for g in range(kv_local):
        where = pl.ds(pl.multiple_of((kv_first + g) * HD, HD), HD)
        part = slice(g * HD, (g + 1) * HD)
        shifted = keys_buf[:, part].astype(jnp.float32) + key_bias_ref[:, where]
        turned = rotate(shifted, cos_ref[...], sin_ref[...]).astype(jnp.bfloat16)
        biased = values_buf[:, part].astype(jnp.float32) + value_bias_ref[:, where]
        biased = biased.astype(jnp.bfloat16)
        kv_ref[0, g] = turned
        kv_ref[1, g] = biased


def turn(dims, positions, key_bias, value_bias, keys, values):
    kv_local, head_count, rows, rep_size = dims
    return pl.pallas_call(
        functools.partial(turn_kernel, dims),
        out_shape=[
            jax.ShapeDtypeStruct((2, kv_local, rows, HD), jnp.bfloat16),
            jax.ShapeDtypeStruct((rows, HD), jnp.float32),
            jax.ShapeDtypeStruct((rows, HD), jnp.float32),
            jax.ShapeDtypeStruct((rows, HD), jnp.int32),
        ],
        in_specs=[VMEM] * 4 + [ANY] * 2,
        out_specs=[VMEM] * 4,
        scratch_shapes=[
            pltpu.VMEM((rows, kv_local * HD), jnp.bfloat16),
            pltpu.VMEM((rows, kv_local * HD), jnp.bfloat16),
            pltpu.SemaphoreType.DMA((2,)),
        ],
        cost_estimate=SMALL,
        name="turn",
    )(
        positions.reshape(-1, HD),
        row_freqs(),
        key_bias.reshape(1, -1),
        value_bias.reshape(1, -1),
        keys,
        values,
    )


def pack_kernel(dims, page_ref, lengths_ref, replica_ref, kv_hbm, cache_hbm, *rest):
    blk_count, group, dec_size = dims
    sends = rest[:dec_size]
    held, valid, counts, in_sems, out_sems = rest[dec_size:]
    pre, dec, rep = lax.axis_index("pre"), lax.axis_index("dec"), lax.axis_index("rep")
    blocks_in = [
        pltpu.make_async_copy(cache_hbm.at[0, b], held.at[b], in_sems.at[b])
        for b in range(blk_count)
    ]
    for copy in blocks_in:
        copy.start()
    blocks_all = valid.shape[0]
    for k in range(blocks_all):
        valid[k] = 0
    for d in range(dec_size):
        counts[d] = 0

    def request(i, start):
        mine = replica_ref[i] == rep
        length = lengths_ref[i]
        number = jnp.where(mine, (length + (BLOCK - 1)) // BLOCK, 0)

        def block(k, carry):
            valid[start + k] = jnp.minimum(BLOCK, length - BLOCK * k)
            return carry

        lax.fori_loop(0, jnp.minimum(number, blocks_all - start), block, 0)
        return start + number

    lax.fori_loop(0, lengths_ref.shape[0], request, 0)
    place = pre * group + dec % group
    lane = lax.broadcasted_iota(jnp.int32, held.shape[1:], len(held.shape) - 2)
    for b in range(blk_count):
        k = pre * blk_count + b
        blocks_in[b].wait()
        limit = valid[k]

        @pl.when(limit < BLOCK)
        def _(b=b, limit=limit):
            held[b] = jnp.where(lane < limit, held[b], jnp.zeros_like(held[b]))

        target = page_ref[rep, k]
        rank = counts[target]
        counts[target] = rank + 1
        for j in range(dec_size):

            @pl.when(target == (place ^ j))
            def _(b=b, j=j, rank=rank):
                pltpu.make_async_copy(held.at[b], sends[j].at[rank], out_sems.at[b]).start()

    for b in range(blk_count):
        pltpu.make_async_copy(held.at[b], sends[0].at[0], out_sems.at[b]).wait()


def pack(dims, capacity, page_table, lengths, replica_of, kv, cache):
    blk_count, group, dec_size = dims
    block = cache.shape[2:]
    return pl.pallas_call(
        functools.partial(pack_kernel, dims),
        out_shape=[jax.ShapeDtypeStruct((capacity,) + block, jnp.bfloat16)] * dec_size,
        in_specs=[SMEM] * 3 + [ANY] * 2,
        out_specs=[ANY] * dec_size,
        scratch_shapes=[
            pltpu.VMEM((blk_count,) + block, jnp.bfloat16),
            pltpu.SMEM((page_table.shape[1],), jnp.int32),
            pltpu.SMEM((dec_size,), jnp.int32),
            pltpu.SemaphoreType.DMA((blk_count,)),
            pltpu.SemaphoreType.DMA((blk_count,)),
        ],
        cost_estimate=SMALL,
        name="pack",
    )(page_table, lengths, replica_of, kv, cache)


def after(value, *before):
    return lax.optimization_barrier((value,) + before)[0] if before else value


def query_kernel(query_ref, bias_ref, cos_ref, sin_ref, out_ref):
    for h in range(out_ref.shape[0]):
        columns = slice(h * HD, (h + 1) * HD)
        shifted = query_ref[:, columns].astype(jnp.float32) + bias_ref[:, columns]
        out_ref[h] = rotate(shifted, cos_ref[...], sin_ref[...]).astype(jnp.bfloat16)


def rotate_queries(queries, bias, cosine, sine):
    rows, columns = queries.shape
    return pl.pallas_call(
        query_kernel,
        out_shape=jax.ShapeDtypeStruct((columns // HD, rows, HD), jnp.bfloat16),
        in_specs=[VMEM] * 4,
        out_specs=VMEM,
        cost_estimate=SMALL,
        name="rotate_queries",
    )(queries, bias.reshape(1, -1), cosine, sine)


def attend_kernel(moves, rep_size, first, last, query_ref, qpos_ref, pos_ref, *rest):
    chunks, rest = rest[: len(moves)], rest[len(moves) :]
    if not first:
        stat_in, sum_in, rest = rest[0], rest[1], rest[2:]
    outs = rest
    step_heads, rows, _ = query_ref.shape
    half = HD // 2
    pre, rep = lax.axis_index("pre"), lax.axis_index("rep")
    scale = HD ** (-0.5) * log2_e
    qpos = qpos_ref[:, :1]
    lanes = lax.broadcasted_iota(jnp.int32, (rows, HD), 1)
    bias, keys, values = [], [], []
    for (move_pre, move_rep), chunk in zip(moves, chunks):
        block = (pre ^ move_pre) * rep_size + (rep ^ move_rep)
        parts = [pos_ref[pl.ds(block * (rows // HD) + r, 1), :] for r in range(rows // HD)]
        bias.append(jnp.concatenate(parts, axis=1) <= qpos)
        keys.append(chunk[0, 0])
        values.append(jnp.concatenate([chunk[1, 0], jnp.ones((rows, HD), jnp.bfloat16)], axis=1))
    stat = jnp.zeros((rows, HD), jnp.float32)
    for h in range(step_heads):
        query = query_ref[h]
        scores = []
        for allowed, key in zip(bias, keys):
            product = lax.dot_general(
                query, key, (((1,), (1,)), ((), ())), preferred_element_type=jnp.float32
            )
            scores.append(jnp.where(allowed, product, masked_score))
        newest = jnp.max(functools.reduce(jnp.maximum, scores), axis=1, keepdims=True)
        if not first:
            best = stat_in[0, :, h : h + 1]
            newest = jnp.maximum(newest, best)
            decay = jnp.exp2((best - newest) * scale)
        both = 0.0
        for score, value in zip(scores, values):
            weights = jnp.exp2((score - newest) * scale)
            both = both + jnp.dot(
                weights.astype(jnp.bfloat16), value, preferred_element_type=jnp.float32
            )
        added, total = both[:, :HD], both[:, HD:]
        if not first:
            total = total + stat_in[0, :, half + h : half + h + 1] * decay
            added = added + sum_in[h] * decay
        if last:
            outs[0][:, h * HD : (h + 1) * HD] = (added / total).astype(jnp.bfloat16)
        else:
            stat = jnp.where(lanes == h, newest, jnp.where(lanes == half + h, total, stat))
            outs[1][h] = added
    if not last:
        outs[0][0] = stat


def attend(pairs, rep_size, per_group, queries, qpos, positions, state, last):
    heads, rows, _ = queries.shape
    step_heads = per_group
    first = state is None
    moves, chunks = zip(*pairs)
    whole = lambda i: (0, 0)
    by_head = pl.BlockSpec((step_heads, rows, HD), lambda i: (i, 0, 0))
    by_step = pl.BlockSpec((1, rows, HD), lambda i: (i, 0, 0))
    chunk_spec = pl.BlockSpec((2, 1, rows, HD), lambda i: (0, i, 0, 0))
    pos2 = positions.reshape(-1, HD)
    in_specs = (
        [by_head, pl.BlockSpec((rows, HD), whole), pl.BlockSpec(pos2.shape, whole)]
        + [chunk_spec] * len(chunks)
        + ([] if first else [by_step, by_head])
    )
    if last:
        out_shape = jax.ShapeDtypeStruct((rows, heads * HD), jnp.bfloat16)
        out_specs = pl.BlockSpec((rows, step_heads * HD), lambda i: (0, i))
    else:
        out_shape = [
            jax.ShapeDtypeStruct((heads // step_heads, rows, HD), jnp.float32),
            jax.ShapeDtypeStruct((heads, rows, HD), jnp.float32),
        ]
        out_specs = [by_step, by_head]
    return pl.pallas_call(
        functools.partial(attend_kernel, moves, rep_size, first, last),
        grid=(heads // step_heads,),
        out_shape=out_shape,
        in_specs=in_specs,
        out_specs=out_specs,
        compiler_params=pltpu.CompilerParams(vmem_limit_bytes=40 << 20),
        cost_estimate=SMALL,
        name="attend",
    )(queries, qpos, pos2, *chunks, *(() if first else state))


def place_kernel(dims, here, rest_j, page_ref, own_hbm, *rest):
    blk_count, capacity, hl, group = dims
    arrived, rest = rest[: len(here)], rest[len(here) :]
    out_hbm, held, zeros, in_sems, out_sems = rest[-5:]
    pre, dec, rep = lax.axis_index("pre"), lax.axis_index("dec"), lax.axis_index("rep")

    def goal(j):
        source = dec ^ j
        run, part = source // group, source % group
        used = functools.reduce(
            jnp.logical_or,
            [page_ref[rep, run * blk_count + b] == dec for b in range(blk_count)],
        )
        return used, lambda c: out_hbm.at[0, 0, run * capacity + c, pl.ds(part * hl, hl)]

    moves = []
    for n, j in enumerate(here):
        used, to = goal(j)
        for c in range(capacity):
            inward = pltpu.make_async_copy(arrived[n].at[c], held.at[n, c], in_sems.at[n, c])
            outward = pltpu.make_async_copy(held.at[n, c], to(c), out_sems.at[n, c])
            moves.append((used, inward, outward))
            local = used & (dec // group == pre) if j == 0 else None
            if j == 0:
                kept = pltpu.make_async_copy(own_hbm.at[c], held.at[n, c], in_sems.at[n, c])

                @pl.when(local)
                def _(kept=kept):
                    kept.start()

            @pl.when(used if local is None else used & jnp.logical_not(local))
            def _(inward=inward):
                inward.start()

    fills = []
    if rest_j:
        zeros[...] = jnp.zeros_like(zeros)
        for n, j in enumerate(rest_j):
            used, to = goal(j)
            for c in range(capacity):
                fill = pltpu.make_async_copy(zeros, to(c), out_sems.at[len(here) + n, c])
                fills.append((used, fill))

                @pl.when(jnp.logical_not(used))
                def _(fill=fill):
                    fill.start()

    for used, inward, outward in moves:

        @pl.when(used)
        def _(inward=inward, outward=outward):
            inward.wait()
            outward.start()

    for used, inward, outward in moves:

        @pl.when(used)
        def _(outward=outward):
            outward.wait()

    for used, fill in fills:

        @pl.when(jnp.logical_not(used))
        def _(fill=fill):
            fill.wait()


def place(dims, pre_size, here, rest_j, page_table, own, arrived, buffer):
    blk_count, capacity, hl, group = dims
    block = arrived[0].shape[2:]
    count = len(here)
    kept = [] if buffer is None else [buffer]
    return pl.pallas_call(
        functools.partial(place_kernel, dims, here, rest_j),
        out_shape=jax.ShapeDtypeStruct((1, 1, pre_size * capacity, group * hl) + block, jnp.bfloat16),
        in_specs=[SMEM] + [ANY] * (1 + count + len(kept)),
        out_specs=ANY,
        scratch_shapes=[
            pltpu.VMEM((count, capacity, hl) + block, jnp.bfloat16),
            pltpu.VMEM((hl,) + block, jnp.bfloat16),
            pltpu.SemaphoreType.DMA((count, capacity)),
            pltpu.SemaphoreType.DMA((count + len(rest_j), capacity)),
        ],
        input_output_aliases={2 + count: 0} if kept else {},
        cost_estimate=SMALL,
        name="place",
    )(page_table, own, *arrived, *kept)


def shards(
    layer_queries,
    layer_keys,
    layer_values,
    query_bias,
    key_bias,
    value_bias,
    positions,
    lengths,
    replica_of,
    page_table,
    prefill_cache,
):
    pre_size, dec_size, rep_size = (lax.axis_size(a) for a in ("pre", "dec", "rep"))
    rows = layer_queries.shape[0]
    head_count = layer_queries.shape[1] // HD
    group_size = HEADS // KVH
    kv_local = max(1, head_count // group_size)
    per_group = head_count // kv_local
    blk_count, hl = prefill_cache.shape[1], prefill_cache.shape[2]
    capacity = 2 * blk_count // dec_size
    group = dec_size // pre_size
    kv, cosine, sine, qpos = turn(
        (kv_local, head_count, rows, rep_size), positions, key_bias, value_bias,
        layer_keys, layer_values,
    )
    sends = pack((blk_count, group, dec_size), capacity, page_table, lengths, replica_of, kv, prefill_cache)
    swap = lambda value, axis, size, hop: lax.ppermute(
        value, axis, [(i, i ^ hop) for i in range(size)]
    )
    near = [kv] + [swap(kv, "pre", pre_size, s) for s in range(1, pre_size)]
    arrived = {}

    def hand_over(j, *before):
        route = []
        for p in range(pre_size):
            for d in range(dec_size):
                goal = (p * group + d % group) ^ j
                pair = (p * dec_size + d, (d // group) * dec_size + goal)
                if pair[0] != pair[1]:
                    route.append(pair)
        arrived[j] = lax.ppermute(after(sends[j], *before), ("pre", "dec"), route)

    order = sorted(range(dec_size), key=lambda j: (j % group, j // group))
    attends = functools.partial(attend, rep_size=rep_size, per_group=per_group, qpos=qpos, positions=positions)
    hops = [1] + list(range(rep_size - 1, 1, -1))
    own = {r: swap(kv, "rep", rep_size, r) for r in hops}
    for j in order[:2]:
        hand_over(j, near[-1])
    for j in order[2:3]:
        hand_over(j, near[-1], own[hops[1]], own[hops[-1]], own[1])
    queries = rotate_queries(layer_queries, query_bias, cosine, sine)
    state = attends([((s, 0), near[s]) for s in range(pre_size)], queries=queries, state=None, last=False)
    far = []
    for r in hops[1:]:
        for s in range(1, pre_size):
            wait = (own[1], state[0]) if r == hops[1] else (own[r], arrived[order[0]])
            far.append(((s, r), swap(after(near[s], *wait), "rep", rep_size, r)))
    for j in order[3:]:
        hand_over(j, near[-1], state[0], own[1], own[hops[-1]])
    for s in range(1, pre_size):
        far.append(((s, 1), swap(after(near[s], own[1], arrived[order[1]]), "rep", rep_size, 1)))
    ready = (after(state[0], arrived[order[0]], arrived[order[1]]), state[1])
    state = attends([((0, r), own[r]) for r in hops], queries=queries, state=ready, last=False)
    state = attends(far, queries=queries, state=state, last=True)
    split = dec_size // 2
    arrange = functools.partial(place, (blk_count, capacity, hl, group), pre_size)
    got = [arrived[j] for j in order]
    decode_cache = arrange(order[:split], order, page_table, sends[0], got[:split], None)
    decode_cache = arrange(
        order[split:], [], page_table, sends[0], got[split:], after(decode_cache, state)
    )
    return (state, decode_cache)


def solution(mesh):
    placed = (
        P(("pre", "rep"), "dec"),
        P(("pre", "rep"), None),
        P(("pre", "rep"), None),
        P("dec"),
        P(),
        P(),
        P(),
        P(),
        P(),
        P(),
        P("rep", "pre", "dec", None, None, None),
    )
    return jax.shard_map(
        shards,
        mesh=mesh,
        in_specs=placed,
        out_specs=(P(("pre", "rep"), "dec"), P("rep", "dec", None, "pre", None, None, None)),
        check_vma=False,
    )
```

```python
import functools

import jax
import jax.numpy as jnp
import numpy as np
from jax import lax
from jax.experimental import pallas as pl
from jax.experimental.pallas import tpu as pltpu
from jax.sharding import PartitionSpec as P

HEADS = 64
KVH = 8
HD = 128
BLOCK = 128

rope_base = 1000000.0
masked_score = -1e30
log2_e = 1.4426950408889634

ANY = pl.BlockSpec(memory_space=pl.ANY)
SMEM = pl.BlockSpec(memory_space=pltpu.SMEM)
VMEM = pl.BlockSpec(memory_space=pltpu.VMEM)
SMALL = pl.CostEstimate(flops=1, bytes_accessed=1, transcendentals=0)


def row_freqs():
    lane = np.arange(HD) % (HD // 2)
    freqs = 1.0 / rope_base ** (lane * (2.0 / HD))
    return jnp.asarray(freqs.astype(np.float32).reshape(1, HD))


def rotate(values, cosine, sine):
    return values * cosine + pltpu.roll(values, HD // 2, 1) * sine


def turn_kernel(
    dims,
    pos_ref,
    freq_ref,
    key_bias_ref,
    value_bias_ref,
    keys_hbm,
    values_hbm,
    kv_ref,
    cos_ref,
    sin_ref,
    qpos_ref,
    keys_buf,
    values_buf,
    sems,
):
    kv_local, head_count, rows, rep_size = dims
    pre, dec, rep = lax.axis_index("pre"), lax.axis_index("dec"), lax.axis_index("rep")
    kv_first = dec * head_count // (HEADS // KVH)
    columns = pl.ds(pl.multiple_of(kv_first * HD, HD), kv_local * HD)
    keys_in = pltpu.make_async_copy(keys_hbm.at[:, columns], keys_buf, sems.at[0])
    values_in = pltpu.make_async_copy(values_hbm.at[:, columns], values_buf, sems.at[1])
    keys_in.start()
    values_in.start()
    first = (pre * rep_size + rep) * (rows // HD)
    lanes = lax.broadcasted_iota(jnp.int32, (HD, HD), 1)
    for r in range(rows // HD):
        part = slice(r * HD, (r + 1) * HD)
        row = pos_ref[pl.ds(first + r, 1), :]
        column = jnp.broadcast_to(row, (HD, HD)).astype(jnp.float32).T
        qpos_ref[part, :] = column.astype(jnp.int32)
        angle = column * freq_ref[...]
        sine = jnp.sin(angle)
        cos_ref[part, :] = jnp.cos(angle)
        sin_ref[part, :] = jnp.where(lanes < HD // 2, -sine, sine)
    keys_in.wait()
    values_in.wait()
    for g in range(kv_local):
        where = pl.ds(pl.multiple_of((kv_first + g) * HD, HD), HD)
        part = slice(g * HD, (g + 1) * HD)
        shifted = keys_buf[:, part].astype(jnp.float32) + key_bias_ref[:, where]
        turned = rotate(shifted, cos_ref[...], sin_ref[...]).astype(jnp.bfloat16)
        biased = values_buf[:, part].astype(jnp.float32) + value_bias_ref[:, where]
        biased = biased.astype(jnp.bfloat16)
        kv_ref[0, g] = turned
        kv_ref[1, g] = biased


def turn(dims, positions, key_bias, value_bias, keys, values):
    kv_local, head_count, rows, rep_size = dims
    return pl.pallas_call(
        functools.partial(turn_kernel, dims),
        out_shape=[
            jax.ShapeDtypeStruct((2, kv_local, rows, HD), jnp.bfloat16),
            jax.ShapeDtypeStruct((rows, HD), jnp.float32),
            jax.ShapeDtypeStruct((rows, HD), jnp.float32),
            jax.ShapeDtypeStruct((rows, HD), jnp.int32),
        ],
        in_specs=[VMEM] * 4 + [ANY] * 2,
        out_specs=[VMEM] * 4,
        scratch_shapes=[
            pltpu.VMEM((rows, kv_local * HD), jnp.bfloat16),
            pltpu.VMEM((rows, kv_local * HD), jnp.bfloat16),
            pltpu.SemaphoreType.DMA((2,)),
        ],
        cost_estimate=SMALL,
        name="turn",
    )(
        positions.reshape(-1, HD),
        row_freqs(),
        key_bias.reshape(1, -1),
        value_bias.reshape(1, -1),
        keys,
        values,
    )


def pack_kernel(dims, page_ref, lengths_ref, replica_ref, kv_hbm, cache_hbm, *rest):
    blk_count, group, dec_size = dims
    sends = rest[:dec_size]
    held, valid, counts, in_sems, out_sems = rest[dec_size:]
    pre, dec, rep = lax.axis_index("pre"), lax.axis_index("dec"), lax.axis_index("rep")
    blocks_in = [
        pltpu.make_async_copy(cache_hbm.at[0, b], held.at[b], in_sems.at[b])
        for b in range(blk_count)
    ]
    for copy in blocks_in:
        copy.start()
    blocks_all = valid.shape[0]
    for k in range(blocks_all):
        valid[k] = 0
    for d in range(dec_size):
        counts[d] = 0

    def request(i, start):
        mine = replica_ref[i] == rep
        length = lengths_ref[i]
        number = jnp.where(mine, (length + (BLOCK - 1)) // BLOCK, 0)

        def block(k, carry):
            valid[start + k] = jnp.minimum(BLOCK, length - BLOCK * k)
            return carry

        lax.fori_loop(0, jnp.minimum(number, blocks_all - start), block, 0)
        return start + number

    lax.fori_loop(0, lengths_ref.shape[0], request, 0)
    place = pre * group + dec % group
    lane = lax.broadcasted_iota(jnp.int32, held.shape[1:], len(held.shape) - 2)
    for b in range(blk_count):
        k = pre * blk_count + b
        blocks_in[b].wait()
        limit = valid[k]

        @pl.when(limit < BLOCK)
        def _(b=b, limit=limit):
            held[b] = jnp.where(lane < limit, held[b], jnp.zeros_like(held[b]))

        target = page_ref[rep, k]
        rank = counts[target]
        counts[target] = rank + 1
        for j in range(dec_size):

            @pl.when(target == (place ^ j))
            def _(b=b, j=j, rank=rank):
                pltpu.make_async_copy(held.at[b], sends[j].at[rank], out_sems.at[b]).start()

    for b in range(blk_count):
        pltpu.make_async_copy(held.at[b], sends[0].at[0], out_sems.at[b]).wait()


def pack(dims, capacity, page_table, lengths, replica_of, kv, cache):
    blk_count, group, dec_size = dims
    block = cache.shape[2:]
    return pl.pallas_call(
        functools.partial(pack_kernel, dims),
        out_shape=[jax.ShapeDtypeStruct((capacity,) + block, jnp.bfloat16)] * dec_size,
        in_specs=[SMEM] * 3 + [ANY] * 2,
        out_specs=[ANY] * dec_size,
        scratch_shapes=[
            pltpu.VMEM((blk_count,) + block, jnp.bfloat16),
            pltpu.SMEM((page_table.shape[1],), jnp.int32),
            pltpu.SMEM((dec_size,), jnp.int32),
            pltpu.SemaphoreType.DMA((blk_count,)),
            pltpu.SemaphoreType.DMA((blk_count,)),
        ],
        cost_estimate=SMALL,
        name="pack",
    )(page_table, lengths, replica_of, kv, cache)


def after(value, *before):
    return lax.optimization_barrier((value,) + before)[0] if before else value


def query_kernel(query_ref, bias_ref, cos_ref, sin_ref, out_ref):
    for h in range(out_ref.shape[0]):
        columns = slice(h * HD, (h + 1) * HD)
        shifted = query_ref[:, columns].astype(jnp.float32) + bias_ref[:, columns]
        out_ref[h] = rotate(shifted, cos_ref[...], sin_ref[...]).astype(jnp.bfloat16)


def rotate_queries(queries, bias, cosine, sine):
    rows, columns = queries.shape
    return pl.pallas_call(
        query_kernel,
        out_shape=jax.ShapeDtypeStruct((columns // HD, rows, HD), jnp.bfloat16),
        in_specs=[VMEM] * 4,
        out_specs=VMEM,
        cost_estimate=SMALL,
        name="rotate_queries",
    )(queries, bias.reshape(1, -1), cosine, sine)


def attend_kernel(moves, rep_size, first, last, query_ref, qpos_ref, pos_ref, *rest):
    chunks, rest = rest[: len(moves)], rest[len(moves) :]
    if not first:
        stat_in, sum_in, rest = rest[0], rest[1], rest[2:]
    outs = rest
    step_heads, rows, _ = query_ref.shape
    half = HD // 2
    pre, rep = lax.axis_index("pre"), lax.axis_index("rep")
    scale = HD ** (-0.5) * log2_e
    qpos = qpos_ref[:, :1]
    lanes = lax.broadcasted_iota(jnp.int32, (rows, HD), 1)
    bias, keys, values = [], [], []
    for (move_pre, move_rep), chunk in zip(moves, chunks):
        block = (pre ^ move_pre) * rep_size + (rep ^ move_rep)
        parts = [pos_ref[pl.ds(block * (rows // HD) + r, 1), :] for r in range(rows // HD)]
        bias.append(jnp.concatenate(parts, axis=1) <= qpos)
        keys.append(chunk[0, 0])
        values.append(jnp.concatenate([chunk[1, 0], jnp.ones((rows, HD), jnp.bfloat16)], axis=1))
    stat = jnp.zeros((rows, HD), jnp.float32)
    for h in range(step_heads):
        query = query_ref[h]
        scores = []
        for allowed, key in zip(bias, keys):
            product = lax.dot_general(
                query, key, (((1,), (1,)), ((), ())), preferred_element_type=jnp.float32
            )
            scores.append(jnp.where(allowed, product, masked_score))
        newest = jnp.max(functools.reduce(jnp.maximum, scores), axis=1, keepdims=True)
        if not first:
            best = stat_in[0, :, h : h + 1]
            newest = jnp.maximum(newest, best)
            decay = jnp.exp2((best - newest) * scale)
        both = 0.0
        for score, value in zip(scores, values):
            weights = jnp.exp2((score - newest) * scale)
            both = both + jnp.dot(
                weights.astype(jnp.bfloat16), value, preferred_element_type=jnp.float32
            )
        added, total = both[:, :HD], both[:, HD:]
        if not first:
            total = total + stat_in[0, :, half + h : half + h + 1] * decay
            added = added + sum_in[h] * decay
        if last:
            outs[0][:, h * HD : (h + 1) * HD] = (added / total).astype(jnp.bfloat16)
        else:
            stat = jnp.where(lanes == h, newest, jnp.where(lanes == half + h, total, stat))
            outs[1][h] = added
    if not last:
        outs[0][0] = stat


def attend(pairs, rep_size, per_group, queries, qpos, positions, state, last):
    heads, rows, _ = queries.shape
    step_heads = per_group
    first = state is None
    moves, chunks = zip(*pairs)
    whole = lambda i: (0, 0)
    by_head = pl.BlockSpec((step_heads, rows, HD), lambda i: (i, 0, 0))
    by_step = pl.BlockSpec((1, rows, HD), lambda i: (i, 0, 0))
    chunk_spec = pl.BlockSpec((2, 1, rows, HD), lambda i: (0, i, 0, 0))
    pos2 = positions.reshape(-1, HD)
    in_specs = (
        [by_head, pl.BlockSpec((rows, HD), whole), pl.BlockSpec(pos2.shape, whole)]
        + [chunk_spec] * len(chunks)
        + ([] if first else [by_step, by_head])
    )
    if last:
        out_shape = jax.ShapeDtypeStruct((rows, heads * HD), jnp.bfloat16)
        out_specs = pl.BlockSpec((rows, step_heads * HD), lambda i: (0, i))
    else:
        out_shape = [
            jax.ShapeDtypeStruct((heads // step_heads, rows, HD), jnp.float32),
            jax.ShapeDtypeStruct((heads, rows, HD), jnp.float32),
        ]
        out_specs = [by_step, by_head]
    return pl.pallas_call(
        functools.partial(attend_kernel, moves, rep_size, first, last),
        grid=(heads // step_heads,),
        out_shape=out_shape,
        in_specs=in_specs,
        out_specs=out_specs,
        compiler_params=pltpu.CompilerParams(vmem_limit_bytes=40 << 20),
        cost_estimate=SMALL,
        name="attend",
    )(queries, qpos, pos2, *chunks, *(() if first else state))


def place_kernel(dims, here, rest_j, page_ref, own_hbm, *rest):
    blk_count, capacity, hl, group = dims
    arrived, rest = rest[: len(here)], rest[len(here) :]
    out_hbm, held, zeros, in_sems, out_sems = rest[-5:]
    pre, dec, rep = lax.axis_index("pre"), lax.axis_index("dec"), lax.axis_index("rep")

    def goal(j):
        source = dec ^ j
        run, part = source // group, source % group
        used = functools.reduce(
            jnp.logical_or,
            [page_ref[rep, run * blk_count + b] == dec for b in range(blk_count)],
        )
        return used, lambda c: out_hbm.at[0, 0, run * capacity + c, pl.ds(part * hl, hl)]

    moves = []
    for n, j in enumerate(here):
        used, to = goal(j)
        for c in range(capacity):
            inward = pltpu.make_async_copy(arrived[n].at[c], held.at[n, c], in_sems.at[n, c])
            outward = pltpu.make_async_copy(held.at[n, c], to(c), out_sems.at[n, c])
            moves.append((used, inward, outward))
            local = used & (dec // group == pre) if j == 0 else None
            if j == 0:
                kept = pltpu.make_async_copy(own_hbm.at[c], held.at[n, c], in_sems.at[n, c])

                @pl.when(local)
                def _(kept=kept):
                    kept.start()

            @pl.when(used if local is None else used & jnp.logical_not(local))
            def _(inward=inward):
                inward.start()

    fills = []
    if rest_j:
        zeros[...] = jnp.zeros_like(zeros)
        for n, j in enumerate(rest_j):
            used, to = goal(j)
            for c in range(capacity):
                fill = pltpu.make_async_copy(zeros, to(c), out_sems.at[len(here) + n, c])
                fills.append((used, fill))

                @pl.when(jnp.logical_not(used))
                def _(fill=fill):
                    fill.start()

    for used, inward, outward in moves:

        @pl.when(used)
        def _(inward=inward, outward=outward):
            inward.wait()
            outward.start()

    for used, inward, outward in moves:

        @pl.when(used)
        def _(outward=outward):
            outward.wait()

    for used, fill in fills:

        @pl.when(jnp.logical_not(used))
        def _(fill=fill):
            fill.wait()


def place(dims, pre_size, here, rest_j, page_table, own, arrived, buffer):
    blk_count, capacity, hl, group = dims
    block = arrived[0].shape[2:]
    count = len(here)
    kept = [] if buffer is None else [buffer]
    return pl.pallas_call(
        functools.partial(place_kernel, dims, here, rest_j),
        out_shape=jax.ShapeDtypeStruct((1, 1, pre_size * capacity, group * hl) + block, jnp.bfloat16),
        in_specs=[SMEM] + [ANY] * (1 + count + len(kept)),
        out_specs=ANY,
        scratch_shapes=[
            pltpu.VMEM((count, capacity, hl) + block, jnp.bfloat16),
            pltpu.VMEM((hl,) + block, jnp.bfloat16),
            pltpu.SemaphoreType.DMA((count, capacity)),
            pltpu.SemaphoreType.DMA((count + len(rest_j), capacity)),
        ],
        input_output_aliases={2 + count: 0} if kept else {},
        cost_estimate=SMALL,
        name="place",
    )(page_table, own, *arrived, *kept)


def shards(
    layer_queries,
    layer_keys,
    layer_values,
    query_bias,
    key_bias,
    value_bias,
    positions,
    lengths,
    replica_of,
    page_table,
    prefill_cache,
):
    pre_size, dec_size, rep_size = (lax.axis_size(a) for a in ("pre", "dec", "rep"))
    rows = layer_queries.shape[0]
    head_count = layer_queries.shape[1] // HD
    group_size = HEADS // KVH
    kv_local = max(1, head_count // group_size)
    per_group = head_count // kv_local
    blk_count, hl = prefill_cache.shape[1], prefill_cache.shape[2]
    capacity = 2 * blk_count // dec_size
    group = dec_size // pre_size
    kv, cosine, sine, qpos = turn(
        (kv_local, head_count, rows, rep_size), positions, key_bias, value_bias,
        layer_keys, layer_values,
    )
    sends = pack((blk_count, group, dec_size), capacity, page_table, lengths, replica_of, kv, prefill_cache)
    swap = lambda value, axis, size, hop: lax.ppermute(
        value, axis, [(i, i ^ hop) for i in range(size)]
    )
    near = [kv] + [swap(kv, "pre", pre_size, s) for s in range(1, pre_size)]
    arrived = {}

    def hand_over(j, *before):
        route = []
        for p in range(pre_size):
            for d in range(dec_size):
                goal = (p * group + d % group) ^ j
                pair = (p * dec_size + d, (d // group) * dec_size + goal)
                if pair[0] != pair[1]:
                    route.append(pair)
        arrived[j] = lax.ppermute(after(sends[j], *before), ("pre", "dec"), route)

    order = sorted(range(dec_size), key=lambda j: (j % group, j // group))
    attends = functools.partial(attend, rep_size=rep_size, per_group=per_group, qpos=qpos, positions=positions)
    hops = [1] + list(range(2, rep_size))
    own = {r: swap(kv, "rep", rep_size, r) for r in hops}
    for j in order[:2]:
        hand_over(j, near[-1])
    for j in order[2:3]:
        hand_over(j, near[-1], own[hops[1]], own[hops[-1]], own[1])
    queries = rotate_queries(layer_queries, query_bias, cosine, sine)
    state = attends([((s, 0), near[s]) for s in range(pre_size)], queries=queries, state=None, last=False)
    far = []
    for r in hops[1:]:
        for s in range(1, pre_size):
            wait = (own[1], state[0]) if r == hops[1] else (own[r], arrived[order[0]])
            far.append(((s, r), swap(after(near[s], *wait), "rep", rep_size, r)))
    for j in order[3:]:
        hand_over(j, near[-1], state[0], own[1], own[hops[-1]])
    for s in range(1, pre_size):
        far.append(((s, 1), swap(after(near[s], own[1], arrived[order[1]]), "rep", rep_size, 1)))
    ready = (after(state[0], arrived[order[0]], arrived[order[1]]), state[1])
    state = attends([((0, r), own[r]) for r in hops], queries=queries, state=ready, last=False)
    state = attends(far, queries=queries, state=state, last=True)
    split = dec_size // 2
    arrange = functools.partial(place, (blk_count, capacity, hl, group), pre_size)
    got = [arrived[j] for j in order]
    decode_cache = arrange(order[:split], order, page_table, sends[0], got[:split], None)
    decode_cache = arrange(
        order[split:], [], page_table, sends[0], got[split:], after(decode_cache, state)
    )
    return (state, decode_cache)


def solution(mesh):
    placed = (
        P(("pre", "rep"), "dec"),
        P(("pre", "rep"), None),
        P(("pre", "rep"), None),
        P("dec"),
        P(),
        P(),
        P(),
        P(),
        P(),
        P(),
        P("rep", "pre", "dec", None, None, None),
    )
    return jax.shard_map(
        shards,
        mesh=mesh,
        in_specs=placed,
        out_specs=(P(("pre", "rep"), "dec"), P("rep", "dec", None, "pre", None, None, None)),
        check_vma=False,
    )
```
